768 devices in a mesh: sx: 24 (over y_lo, z), sy: 32 (over x, y_hi, core).
Axes of the slice: x: 4, y: 8 (y_hi: 4, y_lo: 2; y = y_hi * 2 + y_lo), z: 12, core: 2. Of those that a mesh axis runs over, the one named last changes fastest.
Arguments:
- right_side: float32 [768, 512, 128], P('sx', 'sy'), may hold values from -48 to 48
- class_map: int32 [384, 256, 32], P('sx', 'sy'), may hold values from 0 to 7
- conductivity_table: float32 [8], replicated, may hold values from 0.2 to 5
- velocity: float32 [3, 768, 512, 128], P(None, 'sx', 'sy'), may hold values from -6 to 6
Outputs:
- potential: float32 [768, 512, 128], P('sx', 'sy')
- velocity_next: float32 [3, 768, 512, 128], P(None, ('sx', 'sy'))
The draws below stay inside these ranges and needn't reach their ends.
All inputs are finite; a program needn't handle non-finite values.
Results may differ from the reference program's by a relative error of at most 0.0003.
Values sent between devices are 32-bit elements; how exact they have to be, the bound alone decides.
No kernel may reach another device: no remote copies, remote signals or barrier semaphores. Data moves between devices by JAX's collectives and lax.ppermute only.
A program may use at most 32 MiB of HBM per device.

```python
import math
import jax
import jax.numpy as jnp
from jax import lax

CX = 32
CY = 16
NZ = 128
MARGIN = 4
SWEEPS = 5
CLASSES = 8
NX = 768
NY = 512
N_SX = 24
N_SY = 32


def draw_right_side(key, part):
    cells_x = (jnp.arange(NX).astype(jnp.float32) + 0.5)[:, None, None] / NX
    cells_y = (jnp.arange(NY).astype(jnp.float32) + 0.5)[None, :, None] / NY
    random_part = jnp.clip(jax.random.normal(key, (NX, NY, NZ), jnp.float32), -4.0, 4.0)
    rising = jnp.exp(math.log(3.0) * (cells_x + cells_y))
    return random_part * rising


def plant(values, own_key, low, largest):
    longest = values.shape.index(max(values.shape))
    spots = []
    for shift in (0, 1):
        where = [jax.random.randint(jax.random.fold_in(own_key, axis), (), 0, length) for axis, length in enumerate(values.shape)]
        where[longest] = (where[longest] + shift) % values.shape[longest]
        spots.append(tuple(where))
    return values.at[spots[0]].set(low).at[spots[1]].set(largest)


def block_levels(rng, dims, cuts, smallest, high):
    def one(axis_at, shards_of):
        steps = jax.random.uniform(jax.random.fold_in(jax.random.fold_in(rng, 6), axis_at), (shards_of,), jnp.float32, smallest / len(cuts), high / len(cuts))
        return jnp.repeat(jnp.exp(steps), dims[axis_at] // shards_of).reshape((-1,) + (1,) * (len(dims) - axis_at - 1))

    loudness = one(*cuts[0])
    for cut in cuts[1:]:
        loudness = loudness * one(*cut)
    return loudness


def normal_values(own_key, dims, deviation, reach, pieces=(), kind=jnp.bfloat16):
    values = deviation * jax.random.normal(own_key, dims, jnp.float32)
    if pieces:
        values = values * block_levels(own_key, dims, pieces, -0.22, 0.18)
    return jnp.clip(values, -reach, reach).astype(kind)


def setup_inputs(seed: int = 0) -> dict:
    seeds = jax.random.split(jax.random.key(seed), 5)
    return {
        "right_side": draw_right_side(jax.random.fold_in(seeds[4], 71), 0),
        "class_map": plant(jax.random.randint(seeds[1], (NX // 2, NY // 2, NZ // 4), 0, CLASSES), jax.random.fold_in(seeds[1], 1), 0, CLASSES - 1).astype(jnp.int32),
        "conductivity_table": jnp.clip(jnp.exp(jax.random.uniform(seeds[2], (CLASSES,), jnp.float32, math.log(0.2), math.log(5.0))), 0.2, 5.0),
        "velocity": normal_values(seeds[3], (3, NX, NY, NZ), 1.0, 6.0, ((1, 24), (2, 32)), jnp.float32),
    }


axial_ratio = 0.0625
coupling = 0.25

def spatial_pad(grid_field):
    leading = [(0, 0)] * (grid_field.ndim - 3)
    return jnp.pad(grid_field, leading + [(1, 1), (1, 1), (1, 1)])

def coefficients(cond_padded):
    centre = cond_padded[..., 1:-1, 1:-1, 1:-1]
    face_terms = (0.5 * (centre + cond_padded[..., 2:, 1:-1, 1:-1]), 0.5 * (centre + cond_padded[..., :-2, 1:-1, 1:-1]), 0.5 * (centre + cond_padded[..., 1:-1, 2:, 1:-1]), 0.5 * (centre + cond_padded[..., 1:-1, :-2, 1:-1]), axial_ratio * 0.5 * (centre + cond_padded[..., 1:-1, 1:-1, 2:]), axial_ratio * 0.5 * (centre + cond_padded[..., 1:-1, 1:-1, :-2]))
    diagonal = face_terms[0] + face_terms[1] + face_terms[2] + face_terms[3] + face_terms[4] + face_terms[5]
    return (face_terms, diagonal)

def apply_operator(face_terms, diagonal, padded):
    centre = padded[..., 1:-1, 1:-1, 1:-1]
    beside = face_terms[0] * padded[..., 2:, 1:-1, 1:-1] + face_terms[1] * padded[..., :-2, 1:-1, 1:-1]
    beside = beside + face_terms[2] * padded[..., 1:-1, 2:, 1:-1] + face_terms[3] * padded[..., 1:-1, :-2, 1:-1]
    beside = beside + face_terms[4] * padded[..., 1:-1, 1:-1, 2:] + face_terms[5] * padded[..., 1:-1, 1:-1, :-2]
    return diagonal * centre - beside

def local_sweeps(cond_region, residual_region):
    face_terms, diagonal = coefficients(spatial_pad(cond_region))
    inside = (cond_region > 0.0).astype(jnp.float32)
    inverse = inside / (diagonal + (1.0 - inside))
    update = residual_region * inverse
    for sweep_index in range(SWEEPS - 1):
        update = update + (residual_region - apply_operator(face_terms, diagonal, spatial_pad(update))) * inverse
    return update

def schwarz(conductivity, residual):
    pads = ((MARGIN, MARGIN), (MARGIN, MARGIN), (0, 0))
    wide_cond = jnp.pad(conductivity, pads)
    wide_res = jnp.pad(residual, pads)
    columns = jnp.arange(N_SY, dtype=jnp.int32)[:, None] * CY + jnp.arange(CY + 2 * MARGIN, dtype=jnp.int32)[None, :]

    def one_row(block_index):
        row_start = (block_index * CX).astype(jnp.int32)
        rows_cond = lax.dynamic_slice_in_dim(wide_cond, row_start, CX + 2 * MARGIN, 0)
        rows_res = lax.dynamic_slice_in_dim(wide_res, row_start, CX + 2 * MARGIN, 0)
        region_cond = jnp.moveaxis(rows_cond[:, columns, :], 1, 0)
        region_res = jnp.moveaxis(rows_res[:, columns, :], 1, 0)
        update = local_sweeps(region_cond, region_res)
        own_cells = update[:, MARGIN:MARGIN + CX, MARGIN:MARGIN + CY, :]
        return jnp.moveaxis(own_cells, 0, 1).reshape(CX, NY, NZ)
    blocks = lax.map(one_row, jnp.arange(N_SX, dtype=jnp.int32))
    return blocks.reshape(NX, NY, NZ)

def sine_table(lines_count):
    positions = jnp.arange(lines_count, dtype=jnp.int32) + 1
    phase_index = positions[:, None] * positions[None, :] % (2 * (lines_count + 1))
    return jnp.sqrt(2.0 / (lines_count + 1)) * jnp.sin(jnp.pi * phase_index.astype(jnp.float32) / (lines_count + 1))

def diffusion_gain(lines_count, cells_side):
    positions = (jnp.arange(lines_count, dtype=jnp.int32) + 1).astype(jnp.float32)
    half_sine = jnp.sin(0.5 * jnp.pi * positions / (lines_count + 1))
    stiffness = 8.0 * cells_side * cells_side * half_sine * half_sine
    return (1.0 - stiffness) / (1.0 + stiffness)

def reference(right_side, class_map, conductivity_table, velocity):
    block_values = conductivity_table[class_map]
    conductivity = jnp.repeat(jnp.repeat(jnp.repeat(block_values, 2, axis=0), 2, axis=1), 4, axis=2)
    own_faces, own_diagonal = coefficients(spatial_pad(conductivity))

    def operate(grid_field):
        return apply_operator(own_faces, own_diagonal, spatial_pad(grid_field))
    residual = right_side
    first_dir = schwarz(conductivity, residual)
    image_one = operate(first_dir)
    weight_one = jnp.sum(image_one * image_one)
    alpha_one = jnp.sum(residual * image_one) / weight_one
    residual = residual - alpha_one * image_one
    second_dir = schwarz(conductivity, residual)
    image_two = operate(second_dir)
    beta_two = jnp.sum(image_two * image_one) / weight_one
    image_two = image_two - beta_two * image_one
    second_dir = second_dir - beta_two * first_dir
    alpha_two = jnp.sum(residual * image_two) / jnp.sum(image_two * image_two)
    potential = alpha_one * first_dir
    potential = potential + alpha_two * second_dir
    padded = spatial_pad(potential)
    grad_x = 0.5 * (padded[2:, 1:-1, 1:-1] - padded[:-2, 1:-1, 1:-1])
    grad_y = 0.5 * (padded[1:-1, 2:, 1:-1] - padded[1:-1, :-2, 1:-1])
    force_x = conductivity * (-grad_y - velocity[0])
    force_y = conductivity * (grad_x - velocity[1])
    moved_velocity = jnp.stack([velocity[0] + coupling * force_x, velocity[1] + coupling * force_y, velocity[2]])
    sine_rows = sine_table(NY)
    line_gain = diffusion_gain(NY, CY)[:, None]
    sine_coeffs = jnp.matmul(sine_rows, moved_velocity, precision=lax.Precision.HIGHEST)
    velocity_next = jnp.matmul(sine_rows, sine_coeffs * line_gain, precision=lax.Precision.HIGHEST)
    return (potential, velocity_next)
```

```python
import functools

import jax
import jax.numpy as jnp
import numpy as np
from jax import lax
from jax.experimental import pallas as pl
from jax.experimental.pallas import tpu as pltpu
from jax.sharding import PartitionSpec as P

CX, CY, NZ = 32, 16, 128
CLASSES = 8
PAD = 12
REACH = 10
WX, WY = CX + 2 * PAD, CY + 2 * PAD
EX = 68
EY = 56
AXIAL = 1.0 / 16.0
COUPLING = 0.25
f32 = jnp.float32
bf16 = jnp.bfloat16


def rows_of_lines(table):
    return table.reshape(CX, NZ)


def lay_out(row):
    return jnp.concatenate([row[0:16], row[8:32], row[24:40]], axis=0)


def gather_owned(row, low):
    return jnp.concatenate(
        [
            row[0:8],
            jnp.where(low, row[8:16], row[16:24]),
            row[24:32],
            jnp.where(low, row[32:40], row[40:48]),
            row[48:56],
        ],
        axis=0,
    )


def up_y(v):
    return pltpu.roll(v, v.shape[0] - 1, 0)


def down_y(v):
    return pltpu.roll(v, 1, 0)


def up_z(v):
    return pltpu.roll(v, v.shape[1] - 1, 1)


def down_z(v):
    return pltpu.roll(v, 1, 1)


def operator_row(s_ref, v_ref, xw, first, last):
    sl = slice(first, last)
    s, v = s_ref[xw, sl, :], v_ref[xw, sl, :]
    lane = lax.broadcasted_iota(jnp.int32, s.shape, 1)
    not_top, not_bottom = lane < NZ - 1, lane > 0
    total = (s + s_ref[xw + 1, sl, :]) * (v - v_ref[xw + 1, sl, :])
    total = total + (s + s_ref[xw - 1, sl, :]) * (v - v_ref[xw - 1, sl, :])
    total = total + (s + up_y(s)) * (v - up_y(v))
    total = total + (s + down_y(s)) * (v - down_y(v))
    axial = (s + jnp.where(not_top, up_z(s), 0.0)) * (v - jnp.where(not_top, up_z(v), 0.0))
    axial = axial + (s + jnp.where(not_bottom, down_z(s), 0.0)) * (
        v - jnp.where(not_bottom, down_z(v), 0.0)
    )
    return 0.5 * total + (0.5 * AXIAL) * axial


def loop(start, stop, body):
    def step(i, carry):
        body(i)
        return carry

    lax.fori_loop(start, stop, step, 0)


def krylov_kernel(
    copies,
    own_ref,
    cond_ref,
    yl_ref,
    yr_ref,
    xl_ref,
    xr_ref,
    spread_ref,
    d1_out,
    e_out,
    s_out,
    sums_out,
    sr,
    sa,
    sw,
    rw,
    d1w,
    i1w,
    ew,
    cxp,
    cxm,
    cyp,
    cym,
    czp,
    czm,
    inv,
    t0,
    ta,
    tb,
):
    sr[0, PAD : PAD + CX, :] = yl_ref[CX : CX + 2, :, :].reshape(CX, NZ)
    sr[1, PAD : PAD + CX, :] = cond_ref[...]
    sr[2, PAD : PAD + CX, :] = yr_ref[CX : CX + 2, :, :].reshape(CX, NZ)
    left_rows = xl_ref[3 * REACH : 3 * REACH + 3, :, :].reshape(48, NZ)
    right_rows = xr_ref[3 * REACH : 3 * REACH + 3, :, :].reshape(48, NZ)
    for k, src in enumerate((1, 0, 2)):
        sr[src, 0:PAD, :] = left_rows[PAD * k : PAD * k + PAD, :]
        sr[src, PAD + CX : WX, :] = right_rows[PAD * k : PAD * k + PAD, :]

    sub = lax.broadcasted_iota(jnp.int32, (8, NZ), 0)
    lane8 = lax.broadcasted_iota(jnp.int32, (8, NZ), 1)
    low8 = sub < 4
    pick = lane8 // 32 == (sub // 2 + 2) % 4

    def spread_rows(cx):
        def wide_row(part, half):
            return jnp.broadcast_to(sr[part, pl.ds(2 * cx + half, 1), :], (8, NZ))

        pairs = (
            (wide_row(0, 0), wide_row(0, 1)),
            (wide_row(0, 1), wide_row(1, 0)),
            (wide_row(1, 0), wide_row(1, 1)),
            (wide_row(1, 1), wide_row(2, 0)),
            (wide_row(2, 0), wide_row(2, 1)),
        )
        for t, (a, b) in enumerate(pairs):
            sa[cx, 8 * t : 8 * t + 8, :] = jnp.where(pick, jnp.where(low8, a, b), 0.0)

    loop(0, WX // 2, spread_rows)
    spread = spread_ref[...]

    def spread_cells(c):
        rest = sa[pl.ds(7 * c, 7), :, :].reshape(7 * WY, NZ)
        out = jnp.zeros((7 * WY, NZ), f32)
        for _ in range(3):
            part = rest.astype(bf16)
            rest = rest - part.astype(f32)
            out = out + jnp.dot(part, spread, preferred_element_type=f32)
        out = out.reshape(7, WY, NZ)
        for k in range(7):
            sw[14 * c + 2 * k, :, :] = out[k]
            sw[14 * c + 2 * k + 1, :, :] = out[k]

    loop(0, 4, spread_cells)

    rw[PAD : PAD + CX, 0:PAD, :] = yl_ref[0:CX, CY - PAD : CY, :]
    rw[PAD : PAD + CX, PAD : PAD + CY, :] = own_ref[...]
    rw[PAD : PAD + CX, PAD + CY : WY, :] = yr_ref[0:CX, 0:PAD, :]
    for ref, at in ((xl_ref, PAD - REACH), (xr_ref, PAD + CX)):
        rw[at : at + REACH, PAD : PAD + CY, :] = ref[0:REACH, :, :]
        rw[at : at + REACH, 0:PAD, :] = ref[REACH : 2 * REACH, CY - PAD : CY, :]
        rw[at : at + REACH, PAD + CY : WY, :] = ref[2 * REACH : 3 * REACH, 0:PAD, :]

    def coefficient_row(e, xw, cut_up=False, cut_down=False):
        s5 = sw[xw]
        lane = lax.broadcasted_iota(jnp.int32, (WY, NZ), 1)
        place = lax.broadcasted_iota(jnp.int32, (EY, NZ), 0)
        zp = AXIAL * (s5 + jnp.where(lane < NZ - 1, up_z(s5), 0.0))
        zm = AXIAL * (s5 + jnp.where(lane > 0, down_z(s5), 0.0))
        axial = lay_out(zp + zm)
        s = lay_out(s5)
        yp = s + jnp.where((place == 15) | (place == 39), 0.0, lay_out(up_y(s5)))
        ym = s + jnp.where((place == 16) | (place == 40), 0.0, lay_out(down_y(s5)))
        xp = s if cut_up else s + lay_out(sw[xw + 1])
        xm = s if cut_down else s + lay_out(sw[xw - 1])
        inverse = jnp.where(s > 0.0, 1.0 / (xp + xm + yp + ym + axial), 0.0)
        cxp[e] = xp * inverse
        cxm[e] = xm * inverse
        cyp[e] = yp * inverse
        cym[e] = ym * inverse
        czp[e] = lay_out(jnp.where(lane < NZ - 1, zp, 0.0)) * inverse
        czm[e] = lay_out(jnp.where(lane > 0, zm, 0.0)) * inverse
        inverse = inverse + inverse
        inv[e] = inverse
        t0[e] = lay_out(rw[xw]) * inverse

    loop(0, 13, lambda e: coefficient_row(e, e + 2))
    coefficient_row(13, 15, cut_up=True)
    coefficient_row(14, 8, cut_down=True)
    loop(15, 53, lambda e: coefficient_row(e, e - 6))
    coefficient_row(53, 47, cut_up=True)
    coefficient_row(54, 40, cut_down=True)
    loop(55, EX, lambda e: coefficient_row(e, e - 14))

    low = lax.broadcasted_iota(jnp.int32, (8, NZ), 0) < 4

    def swept(src, e):
        t = src[e]
        a = t0[e] + cxp[e] * src[e + 1]
        b = cyp[e] * up_y(t) + cym[e] * down_y(t)
        c = czp[e] * up_z(t) + czm[e] * down_z(t)
        return (a + cxm[e] * src[e - 1]) + (b + c)

    def sweep(src, dst, ranges):
        for start, stop, _ in ranges:

            def row(e):
                dst[e] = swept(src, e)

            loop(start, stop, row)

    def last_sweep(src, dst, ranges):
        for start, stop, shift in ranges:

            def row(e, shift=shift):
                dst[e + shift] = gather_owned(swept(src, e), low)

            loop(start, stop, row)

    def ranges(k, skip):
        return (
            (skip + k, 14 - k, 2),
            (14 + k, 54 - k, -6),
            (54 + k, EX - skip - k, -14),
        )

    def precondition(dst, skip):
        sweep(t0, ta, ranges(1, skip))
        sweep(ta, tb, ranges(2, skip))
        sweep(tb, ta, ranges(3, skip))
        last_sweep(ta, dst, ranges(4, skip))

    precondition(d1w, 0)

    def image_row(xw):
        i1w[xw] = operator_row(sw, d1w, xw, 0, WY)

    loop(PAD - 5, PAD + CX + 5, image_row)

    for start, stop, shift in ranges(0, 5):

        def start_row(e, shift=shift):
            t0[e] = lay_out(i1w[e + shift]) * inv[e]

        loop(start, stop, start_row)
    precondition(ew, 5)

    place = lax.broadcasted_iota(jnp.int32, (24, NZ), 0)
    owned = (place >= 4) & (place < 20)

    def products(i, sums):
        xw = i + PAD
        j = jnp.where(owned, operator_row(sw, ew, xw, 8, 32), 0.0)
        i1 = jnp.where(owned, i1w[xw, 8:32, :], 0.0)
        r = rw[xw, 8:32, :]

        def fold(v):
            return v[0:8] + v[8:16] + v[16:24]

        terms = (r * i1, i1 * i1, i1 * j, r * j, j * j)
        return tuple(acc + fold(t) for acc, t in zip(sums, terms))

    zero = jnp.zeros((8, NZ), f32)
    sums = lax.fori_loop(0, CX, products, (zero,) * 5)
    block = zero
    for k, acc in enumerate(sums):
        block = jnp.where(sub == k, jnp.sum(acc, axis=0, keepdims=True), block)
    for k in range(copies):
        sums_out[k] = block
    d1_out[...] = d1w[PAD - 1 : PAD + CX + 1, 8:32, :]
    e_out[...] = ew[PAD - 1 : PAD + CX + 1, 8:32, :]
    s_out[...] = sw[PAD : PAD + CX, 8:32, :]


def krylov(copies, own, cond_rows, yl, yr, xl, xr):
    lane = np.arange(NZ)
    spread = jnp.asarray((lane[:, None] % 32 == lane[None, :] // 4).astype(np.float32), bf16)
    wide = pltpu.VMEM((WX, WY, NZ), f32)
    laid = pltpu.VMEM((EX, EY, NZ), f32)
    return pl.pallas_call(
        functools.partial(krylov_kernel, copies),
        out_shape=(
            jax.ShapeDtypeStruct((CX + 2, 24, NZ), f32),
            jax.ShapeDtypeStruct((CX + 2, 24, NZ), f32),
            jax.ShapeDtypeStruct((CX, 24, NZ), f32),
            jax.ShapeDtypeStruct((copies, 8, NZ), f32),
        ),
        scratch_shapes=[
            pltpu.VMEM((3, WX, NZ), f32),
            pltpu.VMEM((WX // 2, WY, NZ), f32),
            wide,
            wide,
            wide,
            wide,
            wide,
        ]
        + [laid] * 10,
        compiler_params=pltpu.CompilerParams(vmem_limit_bytes=48 << 20),
        name="krylov",
    )(own, cond_rows, yl, yr, xl, xr, spread)


def partial_kernel(copies, parts_ref, out_ref):
    total = jnp.sum(parts_ref[...], axis=0)
    for k in range(copies):
        out_ref[k] = total


def partial_sums(parts, copies):
    return pl.pallas_call(
        functools.partial(partial_kernel, copies),
        out_shape=jax.ShapeDtypeStruct((copies, 8, NZ), f32),
        name="partial_sums",
    )(parts)


def velocity_kernel(parts_ref, d1_ref, e_ref, s_ref, v_ref, pot_ref, moved_ref):
    lanes = jnp.sum(jnp.sum(parts_ref[...], axis=0), axis=1, keepdims=True)
    a, b, c, d, g = (lanes[k : k + 1, 0:1] for k in range(5))
    ratio = c / b
    second = (d - ratio * a) / (g - ratio * c)
    first = a / b - ratio * second
    p1 = jnp.broadcast_to(first, (24, NZ))
    p2 = jnp.broadcast_to(second, (24, NZ))

    def row(i, before_here):
        before, here = before_here
        after = p1 * d1_ref[i + 2] + p2 * e_ref[i + 2]
        factor = COUPLING * s_ref[i]
        grad_x = 0.5 * (after - before)
        grad_y = 0.5 * (up_y(here) - down_y(here))
        pot_ref[i] = here[4:20]
        vx, vy = v_ref[0, i], v_ref[1, i]
        force_y = (factor * grad_x)[4:20]
        force_x = (factor * grad_y)[4:20]
        factor = factor[4:20]
        moved_ref[i, 0] = vx - force_x - factor * vx
        moved_ref[i, 1] = vy + force_y - factor * vy
        moved_ref[i, 2] = v_ref[2, i]
        return here, after

    lax.fori_loop(
        0, CX, row, (p1 * d1_ref[0] + p2 * e_ref[0], p1 * d1_ref[1] + p2 * e_ref[1])
    )


def velocity_step(parts, d1, e, cond, velocity):
    return pl.pallas_call(
        velocity_kernel,
        out_shape=(
            jax.ShapeDtypeStruct((CX, CY, NZ), f32),
            jax.ShapeDtypeStruct((CX, 3, CY, NZ), f32),
        ),
        compiler_params=pltpu.CompilerParams(vmem_limit_bytes=32 << 20),
        name="velocity_step",
    )(parts, d1, e, cond, velocity)


def diffusion_matrix(lines_count, cells_side):
    k = np.arange(lines_count) + 1
    phase = (k[:, None] * k[None, :]) % (2 * (lines_count + 1))
    sine = np.sqrt(2.0 / (lines_count + 1)) * np.sin(np.pi * phase / (lines_count + 1))
    half = np.sin(0.5 * np.pi * k / (lines_count + 1))
    gain = 2.0 / (1.0 + 8.0 * cells_side * cells_side * half * half)
    return (sine * gain) @ sine


def diffusion_kernel(high_ref, low_ref, x_ref, out_ref):
    high, low = high_ref[...], low_ref[...]
    for i in range(x_ref.shape[1]):
        for c in range(3):
            x = x_ref[:, i, c, :, :].reshape(high.shape[0], NZ)
            big = x.astype(bf16)
            small = (x - big.astype(f32)).astype(bf16)
            total = jnp.dot(high, small, preferred_element_type=f32)
            total = total + jnp.dot(low, big, preferred_element_type=f32)
            total = total + jnp.dot(high, big, preferred_element_type=f32)
            out_ref[c, i] = total - x


def diffuse(lines, cells_side):
    sources, count = lines.shape[0], lines.shape[1]
    length = sources * cells_side
    matrix = diffusion_matrix(length, cells_side).astype(np.float32)
    high = matrix.astype(bf16)
    low = (matrix - high.astype(np.float32)).astype(bf16)
    return pl.pallas_call(
        diffusion_kernel,
        out_shape=jax.ShapeDtypeStruct((3, count, length, NZ), f32),
        compiler_params=pltpu.CompilerParams(vmem_limit_bytes=32 << 20),
        name="diffuse",
    )(jnp.asarray(high), jnp.asarray(low), lines)


def per_device(right_side, class_map, conductivity_table, velocity):
    nx, ny = lax.axis_size("sx"), lax.axis_size("sy")

    def up(peers):
        return [(i, i + 1) for i in range(peers - 1)]

    def down(peers):
        return [(i + 1, i) for i in range(peers - 1)]

    classes = rows_of_lines(class_map)
    cond_rows = jnp.zeros((CX, NZ), f32)
    for k in range(CLASSES):
        cond_rows = jnp.where(classes == k, conductivity_table[k], cond_rows)
    message = jnp.concatenate([right_side, cond_rows.reshape(2, CY, NZ)], axis=0)
    yl = lax.ppermute(message, "sy", up(ny))
    yr = lax.ppermute(message, "sy", down(ny))

    def strip(at, cond_at):
        rows = [m[at : at + REACH] for m in (right_side, yl, yr)]
        cond = [cond_rows] + [m[CX : CX + 2].reshape(CX, NZ) for m in (yl, yr)]
        cond = [c[cond_at : cond_at + PAD] for c in cond] + [jnp.zeros((12, NZ), f32)]
        return jnp.concatenate(rows + [jnp.concatenate(cond, 0).reshape(3, CY, NZ)], axis=0)

    xl = lax.ppermute(strip(CX - REACH, CX - PAD), "sx", up(nx))
    xr = lax.ppermute(strip(0, 0), "sx", down(nx))
    d1, e, cond, sums = krylov(ny, right_side, cond_rows, yl, yr, xl, xr)
    sums = lax.all_to_all(sums, "sy", split_axis=0, concat_axis=0, tiled=True)
    sums = partial_sums(sums, nx)
    sums = lax.all_to_all(sums, "sx", split_axis=0, concat_axis=0, tiled=True)
    potential, moved = velocity_step(sums, d1, e, cond, velocity)
    lines = lax.all_to_all(
        moved.reshape(ny, CX // ny, 3, CY, NZ), "sy", split_axis=0, concat_axis=0, tiled=True
    )
    return potential, diffuse(lines, CY)


def solution(mesh):
    return jax.shard_map(
        per_device,
        mesh=mesh,
        in_specs=(P("sx", "sy", None), P("sx", "sy", None), P(), P(None, "sx", "sy", None)),
        out_specs=(P("sx", "sy", None), P(None, ("sx", "sy"), None, None)),
        check_vma=False,
    )
```

```python
import functools

import jax
import jax.numpy as jnp
import numpy as np
from jax import lax
from jax.experimental import pallas as pl
from jax.experimental.pallas import tpu as pltpu
from jax.sharding import PartitionSpec as P

CX, CY, NZ = 32, 16, 128
CLASSES = 8
PAD = 12
REACH = 10
WX, WY = CX + 2 * PAD, CY + 2 * PAD
EX = 68
EY = 56
AXIAL = 1.0 / 16.0
COUPLING = 0.25
GROUP, GROUP_C, GROUP_I, GROUP_P = 10, 13, 21, 16
f32 = jnp.float32
bf16 = jnp.bfloat16


def lay_out(row):
    return jnp.concatenate([row[0:16], row[8:32], row[24:40]], axis=0)


def gather_owned(row, low):
    return jnp.concatenate(
        [
            row[0:8],
            jnp.where(low, row[8:16], row[16:24]),
            row[24:32],
            jnp.where(low, row[32:40], row[40:48]),
            row[48:56],
        ],
        axis=0,
    )


def up_y(v):
    return pltpu.roll(v, v.shape[0] - 1, 0)


def down_y(v):
    return pltpu.roll(v, 1, 0)


def up_z(v):
    return pltpu.roll(v, v.shape[1] - 1, 1)


def down_z(v):
    return pltpu.roll(v, 1, 1)


def operator_row(s_ref, v_ref, xw, first, last):
    sl = slice(first, last)
    s, v = s_ref[xw, sl, :], v_ref[xw, sl, :]
    lane = lax.broadcasted_iota(jnp.int32, s.shape, 1)
    not_top, not_bottom = lane < NZ - 1, lane > 0
    total = (s + s_ref[xw + 1, sl, :]) * (v - v_ref[xw + 1, sl, :])
    total = total + (s + s_ref[xw - 1, sl, :]) * (v - v_ref[xw - 1, sl, :])
    total = total + (s + up_y(s)) * (v - up_y(v))
    total = total + (s + down_y(s)) * (v - down_y(v))
    axial = (s + jnp.where(not_top, up_z(s), 0.0)) * (v - jnp.where(not_top, up_z(v), 0.0))
    axial = axial + (s + jnp.where(not_bottom, down_z(s), 0.0)) * (
        v - jnp.where(not_bottom, down_z(v), 0.0)
    )
    return 0.5 * total + (0.5 * AXIAL) * axial


def loop(start, stop, body, group=1):
    whole = (stop - start) // group

    def step(k, carry):
        body(start + k * group, group)
        return carry

    if whole > 1:
        lax.fori_loop(0, whole, step, 0)
    elif whole == 1:
        body(start, group)
    if start + whole * group < stop:
        body(start + whole * group, stop - start - whole * group)


def message_kernel(table_ref, side_ref, class_ref, out_ref):
    out_ref[0:CX] = side_ref[...]
    for h in range(2):
        classes = jnp.concatenate([class_ref[:, 4 * h + m, :] for m in range(4)], axis=1)
        cond = jnp.zeros(classes.shape, f32)
        for k in range(CLASSES):
            cond = jnp.where(classes == k, table_ref[k], cond)
        out_ref[CX + h] = cond


def message_of(table, right_side, class_map):
    vmem = pl.BlockSpec(memory_space=pltpu.VMEM)
    return pl.pallas_call(
        message_kernel,
        in_specs=[pl.BlockSpec(memory_space=pltpu.SMEM), vmem, vmem],
        out_shape=jax.ShapeDtypeStruct((CX + 2, CY, NZ), f32),
        name="message",
    )(table, right_side, class_map)


def krylov_kernel(
    copies,
    own_ref,
    yl_ref,
    yr_ref,
    xl_ref,
    xr_ref,
    spread_ref,
    d1_out,
    e_out,
    s_out,
    sums_out,
    sr,
    sa,
    sw,
    rw,
    d1w,
    i1w,
    ew,
    cxp,
    cxm,
    cyp,
    cym,
    czp,
    czm,
    inv,
    t0,
    ta,
    tb,
):
    half = PAD // 2
    for k, ref in enumerate((yl_ref, own_ref, yr_ref)):
        for h in range(2):
            sr[k, h, half : half + CX // 2, :] = ref[CX + h, :, :]
    for k, src in enumerate((1, 0, 2)):
        for h in range(2):
            at = slice(8 * h, 8 * h + half)
            sr[src, h, 0:half, :] = xl_ref[3 * REACH + k, at, :]
            sr[src, h, half + CX // 2 : WX // 2, :] = xr_ref[3 * REACH + k, at, :]

    sub = lax.broadcasted_iota(jnp.int32, (8, NZ), 0)
    lane8 = lax.broadcasted_iota(jnp.int32, (8, NZ), 1)
    low8 = sub < 4
    pick = lane8 // 32 == (sub // 2 + 2) % 4

    def spread_row(cx):
        def wide_row(part, h):
            return jnp.broadcast_to(sr[part, h, pl.ds(cx, 1), :], (8, NZ))

        pairs = (
            (wide_row(0, 0), wide_row(0, 1)),
            (wide_row(0, 1), wide_row(1, 0)),
            (wide_row(1, 0), wide_row(1, 1)),
            (wide_row(1, 1), wide_row(2, 0)),
            (wide_row(2, 0), wide_row(2, 1)),
        )
        for t, (a, b) in enumerate(pairs):
            sa[cx, 8 * t : 8 * t + 8, :] = jnp.where(pick, jnp.where(low8, a, b), 0.0)

    def spread_rows(cx, n):
        for i in range(n):
            spread_row(cx + i)

    loop(0, WX // 2, spread_rows, 4)
    spread = spread_ref[...]

    def spread_cells(c, _):
        rest = sa[pl.ds(7 * c, 7), :, :].reshape(7 * WY, NZ)
        out = jnp.zeros((7 * WY, NZ), f32)
        for _ in range(3):
            part = rest.astype(bf16)
            rest = rest - part.astype(f32)
            out = out + jnp.dot(part, spread, preferred_element_type=f32)
        out = out.reshape(7, WY, NZ)
        for k in range(7):
            sw[14 * c + 2 * k, :, :] = out[k]
            sw[14 * c + 2 * k + 1, :, :] = out[k]

    loop(0, 4, spread_cells)

    rw[PAD : PAD + CX, 0:PAD, :] = yl_ref[0:CX, CY - PAD : CY, :]
    rw[PAD : PAD + CX, PAD : PAD + CY, :] = own_ref[0:CX, :, :]
    rw[PAD : PAD + CX, PAD + CY : WY, :] = yr_ref[0:CX, 0:PAD, :]
    for ref, at in ((xl_ref, PAD - REACH), (xr_ref, PAD + CX)):
        rw[at : at + REACH, PAD : PAD + CY, :] = ref[0:REACH, :, :]
        rw[at : at + REACH, 0:PAD, :] = ref[REACH : 2 * REACH, CY - PAD : CY, :]
        rw[at : at + REACH, PAD + CY : WY, :] = ref[2 * REACH : 3 * REACH, 0:PAD, :]

    def coefficient_row(e, xw, cut_up=False, cut_down=False):
        s5 = sw[xw]
        lane = lax.broadcasted_iota(jnp.int32, (WY, NZ), 1)
        place = lax.broadcasted_iota(jnp.int32, (EY, NZ), 0)
        zp = AXIAL * (s5 + jnp.where(lane < NZ - 1, up_z(s5), 0.0))
        zm = AXIAL * (s5 + jnp.where(lane > 0, down_z(s5), 0.0))
        axial = lay_out(zp + zm)
        s = lay_out(s5)
        yp = s + jnp.where((place == 15) | (place == 39), 0.0, lay_out(up_y(s5)))
        ym = s + jnp.where((place == 16) | (place == 40), 0.0, lay_out(down_y(s5)))
        xp = s if cut_up else s + lay_out(sw[xw + 1])
        xm = s if cut_down else s + lay_out(sw[xw - 1])
        inverse = jnp.where(s > 0.0, 1.0 / (xp + xm + yp + ym + axial), 0.0)
        cxp[e] = xp * inverse
        cxm[e] = xm * inverse
        cyp[e] = yp * inverse
        cym[e] = ym * inverse
        czp[e] = lay_out(jnp.where(lane < NZ - 1, zp, 0.0)) * inverse
        czm[e] = lay_out(jnp.where(lane > 0, zm, 0.0)) * inverse
        inverse = inverse + inverse
        inv[e] = inverse
        t0[e] = lay_out(rw[xw]) * inverse

    def coefficient_rows(shift):
        def rows(e, n):
            for i in range(n):
                coefficient_row(e + i, e + i + shift)

        return rows

    loop(0, 13, coefficient_rows(2), GROUP_C)
    coefficient_row(13, 15, cut_up=True)
    coefficient_row(14, 8, cut_down=True)
    loop(15, 53, coefficient_rows(-6), GROUP_C)
    coefficient_row(53, 47, cut_up=True)
    coefficient_row(54, 40, cut_down=True)
    loop(55, EX, coefficient_rows(-14), GROUP_C)

    low = lax.broadcasted_iota(jnp.int32, (8, NZ), 0) < 4

    def swept(src, e, n):
        rows = [src[e - 1 + i] for i in range(n + 2)]
        out = []
        for i in range(n):
            t = rows[i + 1]
            a = t0[e + i] + cxp[e + i] * rows[i + 2]
            b = cyp[e + i] * up_y(t) + cym[e + i] * down_y(t)
            c = czp[e + i] * up_z(t) + czm[e + i] * down_z(t)
            out.append((a + cxm[e + i] * rows[i]) + (b + c))
        return out

    def sweep(src, dst, ranges):
        def rows(e, n):
            for i, new in enumerate(swept(src, e, n)):
                dst[e + i] = new

        for start, stop, _ in ranges:
            loop(start, stop, rows, GROUP)

    def last_sweep(src, dst, ranges):
        for start, stop, shift in ranges:

            def rows(e, n, shift=shift):
                for i, new in enumerate(swept(src, e, n)):
                    dst[e + shift + i] = gather_owned(new, low)

            loop(start, stop, rows, GROUP)

    def ranges(k, skip):
        return (
            (skip + k, 14 - k, 2),
            (14 + k, 54 - k, -6),
            (54 + k, EX - skip - k, -14),
        )

    def precondition(dst, skip):
        sweep(t0, ta, ranges(1, skip))
        sweep(ta, tb, ranges(2, skip))
        sweep(tb, ta, ranges(3, skip))
        last_sweep(ta, dst, ranges(4, skip))

    precondition(d1w, 0)

    def image_rows(xw, n):
        for i, new in enumerate([operator_row(sw, d1w, xw + i, 0, WY) for i in range(n)]):
            i1w[xw + i] = new

    loop(PAD - 5, PAD + CX + 5, image_rows, GROUP_I)

    for start, stop, shift in ranges(0, 5):

        def start_rows(e, n, shift=shift):
            for i in range(n):
                t0[e + i] = lay_out(i1w[e + shift + i]) * inv[e + i]

        loop(start, stop, start_rows, 4)
    precondition(ew, 5)

    place = lax.broadcasted_iota(jnp.int32, (24, NZ), 0)
    owned = (place >= 4) & (place < 20)

    def products(xw, sums):
        j = jnp.where(owned, operator_row(sw, ew, xw, 8, 32), 0.0)
        i1 = jnp.where(owned, i1w[xw, 8:32, :], 0.0)
        r = rw[xw, 8:32, :]

        def fold(v):
            return v[0:8] + v[8:16] + v[16:24]

        terms = (r * i1, i1 * i1, i1 * j, r * j, j * j)
        return tuple(acc + fold(t) for acc, t in zip(sums, terms))

    def product_rows(k, sums):
        for i in range(GROUP_P):
            sums = products(PAD + GROUP_P * k + i, sums)
        return sums

    zero = jnp.zeros((8, NZ), f32)
    sums = lax.fori_loop(0, CX // GROUP_P, product_rows, (zero,) * 5)
    block = jnp.zeros((1, NZ), f32)
    for k, acc in enumerate(sums):
        total = jnp.sum(jnp.sum(acc, axis=0, keepdims=True), axis=1, keepdims=True)
        block = jnp.where(lane8[0:1] == k, total, block)
    for k in range(copies):
        sums_out[k] = block
    d1_out[...] = d1w[PAD - 1 : PAD + CX + 1, 8:32, :]
    e_out[...] = ew[PAD - 1 : PAD + CX + 1, 8:32, :]
    s_out[...] = sw[PAD : PAD + CX, 8:32, :]


def krylov(copies, own, yl, yr, xl, xr):
    lane = np.arange(NZ)
    spread = jnp.asarray((lane[:, None] % 32 == lane[None, :] // 4).astype(np.float32), bf16)
    wide = pltpu.VMEM((WX, WY, NZ), f32)
    laid = pltpu.VMEM((EX, EY, NZ), f32)
    return pl.pallas_call(
        functools.partial(krylov_kernel, copies),
        out_shape=(
            jax.ShapeDtypeStruct((CX + 2, 24, NZ), f32),
            jax.ShapeDtypeStruct((CX + 2, 24, NZ), f32),
            jax.ShapeDtypeStruct((CX, 24, NZ), f32),
            jax.ShapeDtypeStruct((copies, 1, NZ), f32),
        ),
        scratch_shapes=[
            pltpu.VMEM((3, 2, WX // 2, NZ), f32),
            pltpu.VMEM((WX // 2, WY, NZ), f32),
            wide,
            wide,
            wide,
            wide,
            wide,
        ]
        + [laid] * 10,
        compiler_params=pltpu.CompilerParams(vmem_limit_bytes=48 << 20),
        name="krylov",
    )(own, yl, yr, xl, xr, spread)


def partial_kernel(copies, parts_ref, out_ref):
    total = jnp.sum(parts_ref[...], axis=0)
    for k in range(copies):
        out_ref[k] = total


def partial_sums(parts, copies):
    return pl.pallas_call(
        functools.partial(partial_kernel, copies),
        out_shape=jax.ShapeDtypeStruct((copies, 1, NZ), f32),
        name="partial_sums",
    )(parts)


def velocity_kernel(parts_ref, d1_ref, e_ref, s_ref, v_ref, pot_ref, moved_ref):
    totals = jnp.sum(parts_ref[...], axis=0)
    lane = lax.broadcasted_iota(jnp.int32, (1, NZ), 1)
    a, b, c, d, g = (
        jnp.sum(jnp.where(lane == k, totals, 0.0), axis=1, keepdims=True) for k in range(5)
    )
    ratio = c / b
    second = (d - ratio * a) / (g - ratio * c)
    first = a / b - ratio * second
    p1 = jnp.broadcast_to(first, (24, NZ))
    p2 = jnp.broadcast_to(second, (24, NZ))

    def row(i, before_here):
        before, here = before_here
        after = p1 * d1_ref[i + 2] + p2 * e_ref[i + 2]
        factor = COUPLING * s_ref[i]
        grad_x = 0.5 * (after - before)
        grad_y = 0.5 * (up_y(here) - down_y(here))
        pot_ref[i] = here[4:20]
        vx, vy = v_ref[0, i], v_ref[1, i]
        force_y = (factor * grad_x)[4:20]
        force_x = (factor * grad_y)[4:20]
        factor = factor[4:20]
        moved_ref[i, 0] = vx - force_x - factor * vx
        moved_ref[i, 1] = vy + force_y - factor * vy
        moved_ref[i, 2] = v_ref[2, i]
        return here, after

    lax.fori_loop(
        0, CX, row, (p1 * d1_ref[0] + p2 * e_ref[0], p1 * d1_ref[1] + p2 * e_ref[1])
    )


def velocity_step(parts, d1, e, cond, velocity):
    return pl.pallas_call(
        velocity_kernel,
        out_shape=(
            jax.ShapeDtypeStruct((CX, CY, NZ), f32),
            jax.ShapeDtypeStruct((CX, 3, CY, NZ), f32),
        ),
        compiler_params=pltpu.CompilerParams(vmem_limit_bytes=32 << 20),
        name="velocity_step",
    )(parts, d1, e, cond, velocity)


def diffusion_matrix(lines_count, cells_side):
    k = np.arange(lines_count) + 1
    phase = (k[:, None] * k[None, :]) % (2 * (lines_count + 1))
    sine = np.sqrt(2.0 / (lines_count + 1)) * np.sin(np.pi * phase / (lines_count + 1))
    half = np.sin(0.5 * np.pi * k / (lines_count + 1))
    gain = 2.0 / (1.0 + 8.0 * cells_side * cells_side * half * half)
    return (sine * gain) @ sine


def diffusion_kernel(high_ref, low_ref, x_ref, out_ref):
    high, low = high_ref[...], low_ref[...]
    for i in range(x_ref.shape[1]):
        for c in range(3):
            x = x_ref[:, i, c, :, :].reshape(high.shape[0], NZ)
            big = x.astype(bf16)
            small = (x - big.astype(f32)).astype(bf16)
            total = jnp.dot(high, small, preferred_element_type=f32)
            total = total + jnp.dot(low, big, preferred_element_type=f32)
            total = total + jnp.dot(high, big, preferred_element_type=f32)
            out_ref[c, i] = total - x


def diffuse(lines, cells_side):
    sources, count = lines.shape[0], lines.shape[1]
    length = sources * cells_side
    matrix = diffusion_matrix(length, cells_side).astype(np.float32)
    high = matrix.astype(bf16)
    low = (matrix - high.astype(np.float32)).astype(bf16)
    return pl.pallas_call(
        diffusion_kernel,
        out_shape=jax.ShapeDtypeStruct((3, count, length, NZ), f32),
        compiler_params=pltpu.CompilerParams(vmem_limit_bytes=32 << 20),
        name="diffuse",
    )(jnp.asarray(high), jnp.asarray(low), lines)


def per_device(right_side, class_map, conductivity_table, velocity):
    nx, ny = lax.axis_size("sx"), lax.axis_size("sy")

    def up(peers):
        return [(i, i + 1) for i in range(peers - 1)]

    def down(peers):
        return [(i + 1, i) for i in range(peers - 1)]

    own = message_of(conductivity_table, right_side, class_map)
    yl = lax.ppermute(own, "sy", up(ny))
    yr = lax.ppermute(own, "sy", down(ny))

    def strip(at, cond_at):
        parts = (own, yl, yr)
        cond = [m[CX : CX + 2, cond_at : cond_at + PAD // 2] for m in parts]
        cond = jnp.pad(jnp.stack(cond), ((0, 0), (0, 0), (0, 2), (0, 0)))
        rows = [m[at : at + REACH] for m in parts]
        return jnp.concatenate(rows + [cond.reshape(3, CY, NZ)], axis=0)

    xl = lax.ppermute(strip(CX - REACH, CX // 2 - PAD // 2), "sx", up(nx))
    xr = lax.ppermute(strip(0, 0), "sx", down(nx))
    d1, e, cond, sums = krylov(ny, own, yl, yr, xl, xr)
    sums = lax.all_to_all(sums, "sy", split_axis=0, concat_axis=0, tiled=True)
    sums = partial_sums(sums, nx)
    sums = lax.all_to_all(sums, "sx", split_axis=0, concat_axis=0, tiled=True)
    potential, moved = velocity_step(sums, d1, e, cond, velocity)
    lines = lax.all_to_all(
        moved.reshape(ny, CX // ny, 3, CY, NZ), "sy", split_axis=0, concat_axis=0, tiled=True
    )
    return potential, diffuse(lines, CY)


def solution(mesh):
    return jax.shard_map(
        per_device,
        mesh=mesh,
        in_specs=(P("sx", "sy", None), P("sx", "sy", None), P(), P(None, "sx", "sy", None)),
        out_specs=(P("sx", "sy", None), P(None, ("sx", "sy"), None, None)),
        check_vma=False,
    )
```

```python
import functools

import jax
import jax.numpy as jnp
import numpy as np
from jax import lax
from jax.experimental import pallas as pl
from jax.experimental.pallas import tpu as pltpu
from jax.sharding import PartitionSpec as P

CX, CY, NZ = 32, 16, 128
CLASSES = 8
PAD = 12
REACH = 10
WX, WY = CX + 2 * PAD, CY + 2 * PAD
EX = 68
EY = 56
AXIAL = 1.0 / 16.0
COUPLING = 0.25
GROUP, GROUP_C, GROUP_I, GROUP_P = 19, 13, 21, 16
f32 = jnp.float32
bf16 = jnp.bfloat16


def lay_out(row):
    return jnp.concatenate([row[0:16], row[8:32], row[24:40]], axis=0)


def gather_middle(row, low):
    return jnp.concatenate(
        [
            jnp.where(low, row[0:8], row[8:16]),
            row[16:24],
            jnp.where(low, row[24:32], row[32:40]),
        ],
        axis=0,
    )


def gather_owned(row, low):
    return jnp.concatenate([row[0:8], gather_middle(row[8:48], low), row[48:56]], axis=0)


def up_y(v):
    return pltpu.roll(v, v.shape[0] - 1, 0)


def down_y(v):
    return pltpu.roll(v, 1, 0)


def up_z(v):
    return pltpu.roll(v, v.shape[1] - 1, 1)


def down_z(v):
    return pltpu.roll(v, 1, 1)


def operator_row(s_ref, v_ref, xw, first, last):
    sl = slice(first, last)
    s, v = s_ref[xw, sl, :], v_ref[xw, sl, :]
    lane = lax.broadcasted_iota(jnp.int32, s.shape, 1)
    not_top, not_bottom = lane < NZ - 1, lane > 0
    total = (s + s_ref[xw + 1, sl, :]) * (v - v_ref[xw + 1, sl, :])
    total = total + (s + s_ref[xw - 1, sl, :]) * (v - v_ref[xw - 1, sl, :])
    total = total + (s + up_y(s)) * (v - up_y(v))
    total = total + (s + down_y(s)) * (v - down_y(v))
    axial = (s + jnp.where(not_top, up_z(s), 0.0)) * (v - jnp.where(not_top, up_z(v), 0.0))
    axial = axial + (s + jnp.where(not_bottom, down_z(s), 0.0)) * (
        v - jnp.where(not_bottom, down_z(v), 0.0)
    )
    return 0.5 * total + (0.5 * AXIAL) * axial


def loop(start, stop, body, group=1):
    whole = (stop - start) // group

    def step(k, carry):
        body(start + k * group, group)
        return carry

    if whole > 1:
        lax.fori_loop(0, whole, step, 0)
    elif whole == 1:
        body(start, group)
    if start + whole * group < stop:
        body(start + whole * group, stop - start - whole * group)


def message_kernel(table_ref, side_ref, class_ref, out_ref):
    out_ref[0:CX] = side_ref[...]
    for h in range(2):
        classes = jnp.concatenate([class_ref[:, 4 * h + m, :] for m in range(4)], axis=1)
        cond = jnp.zeros(classes.shape, f32)
        for k in range(CLASSES):
            cond = jnp.where(classes == k, table_ref[k], cond)
        out_ref[CX + h] = cond


def message_of(table, right_side, class_map):
    vmem = pl.BlockSpec(memory_space=pltpu.VMEM)
    return pl.pallas_call(
        message_kernel,
        in_specs=[pl.BlockSpec(memory_space=pltpu.SMEM), vmem, vmem],
        out_shape=jax.ShapeDtypeStruct((CX + 2, CY, NZ), f32),
        name="message",
    )(table, right_side, class_map)


def krylov_kernel(
    copies,
    own_ref,
    yl_ref,
    yr_ref,
    xl_ref,
    xr_ref,
    spread_ref,
    d1_out,
    e_out,
    s_out,
    sums_out,
    sr,
    sa,
    sw,
    rw,
    d1w,
    i1w,
    ew,
    cxp,
    cxm,
    cyp,
    cym,
    czp,
    czm,
    inv,
    t0,
    ta,
    tb,
):
    half = PAD // 2
    for k, ref in enumerate((yl_ref, own_ref, yr_ref)):
        for h in range(2):
            sr[k, h, half : half + CX // 2, :] = ref[CX + h, :, :]
    for k, src in enumerate((1, 0, 2)):
        for h in range(2):
            at = slice(8 * h, 8 * h + half)
            sr[src, h, 0:half, :] = xl_ref[3 * REACH + k, at, :]
            sr[src, h, half + CX // 2 : WX // 2, :] = xr_ref[3 * REACH + k, at, :]

    sub = lax.broadcasted_iota(jnp.int32, (8, NZ), 0)
    lane8 = lax.broadcasted_iota(jnp.int32, (8, NZ), 1)
    low8 = sub < 4
    pick = lane8 // 32 == (sub // 2 + 2) % 4

    def spread_row(cx):
        def wide_row(part, h):
            return jnp.broadcast_to(sr[part, h, pl.ds(cx, 1), :], (8, NZ))

        pairs = (
            (wide_row(0, 0), wide_row(0, 1)),
            (wide_row(0, 1), wide_row(1, 0)),
            (wide_row(1, 0), wide_row(1, 1)),
            (wide_row(1, 1), wide_row(2, 0)),
            (wide_row(2, 0), wide_row(2, 1)),
        )
        for t, (a, b) in enumerate(pairs):
            sa[cx, 8 * t : 8 * t + 8, :] = jnp.where(pick, jnp.where(low8, a, b), 0.0)

    def spread_rows(cx, n):
        for i in range(n):
            spread_row(cx + i)

    loop(0, WX // 2, spread_rows, 4)
    spread = spread_ref[...]

    def spread_cells(c, _):
        rest = sa[pl.ds(7 * c, 7), :, :].reshape(7 * WY, NZ)
        out = jnp.zeros((7 * WY, NZ), f32)
        for _ in range(3):
            part = rest.astype(bf16)
            rest = rest - part.astype(f32)
            out = out + jnp.dot(part, spread, preferred_element_type=f32)
        out = out.reshape(7, WY, NZ)
        for k in range(7):
            sw[14 * c + 2 * k, :, :] = out[k]
            sw[14 * c + 2 * k + 1, :, :] = out[k]

    loop(0, 4, spread_cells)

    rw[PAD : PAD + CX, 0:PAD, :] = yl_ref[0:CX, CY - PAD : CY, :]
    rw[PAD : PAD + CX, PAD : PAD + CY, :] = own_ref[0:CX, :, :]
    rw[PAD : PAD + CX, PAD + CY : WY, :] = yr_ref[0:CX, 0:PAD, :]
    for ref, at in ((xl_ref, PAD - REACH), (xr_ref, PAD + CX)):
        rw[at : at + REACH, PAD : PAD + CY, :] = ref[0:REACH, :, :]
        rw[at : at + REACH, 0:PAD, :] = ref[REACH : 2 * REACH, CY - PAD : CY, :]
        rw[at : at + REACH, PAD + CY : WY, :] = ref[2 * REACH : 3 * REACH, 0:PAD, :]

    def coefficient_row(e, xw, cut_up=False, cut_down=False):
        s5 = sw[xw]
        lane = lax.broadcasted_iota(jnp.int32, (WY, NZ), 1)
        place = lax.broadcasted_iota(jnp.int32, (EY, NZ), 0)
        zp = AXIAL * (s5 + jnp.where(lane < NZ - 1, up_z(s5), 0.0))
        zm = AXIAL * (s5 + jnp.where(lane > 0, down_z(s5), 0.0))
        axial = lay_out(zp + zm)
        s = lay_out(s5)
        yp = s + jnp.where((place == 15) | (place == 39), 0.0, lay_out(up_y(s5)))
        ym = s + jnp.where((place == 16) | (place == 40), 0.0, lay_out(down_y(s5)))
        xp = s if cut_up else s + lay_out(sw[xw + 1])
        xm = s if cut_down else s + lay_out(sw[xw - 1])
        inverse = jnp.where(s > 0.0, 1.0 / (xp + xm + yp + ym + axial), 0.0)
        cxp[e] = xp * inverse
        cxm[e] = xm * inverse
        cyp[e] = yp * inverse
        cym[e] = ym * inverse
        czp[e] = lay_out(jnp.where(lane < NZ - 1, zp, 0.0)) * inverse
        czm[e] = lay_out(jnp.where(lane > 0, zm, 0.0)) * inverse
        inverse = inverse + inverse
        inv[e] = inverse
        t0[e] = lay_out(rw[xw]) * inverse

    def coefficient_rows(shift):
        def rows(e, n):
            for i in range(n):
                coefficient_row(e + i, e + i + shift)

        return rows

    loop(0, 13, coefficient_rows(2), GROUP_C)
    coefficient_row(13, 15, cut_up=True)
    coefficient_row(14, 8, cut_down=True)
    loop(15, 53, coefficient_rows(-6), GROUP_C)
    coefficient_row(53, 47, cut_up=True)
    coefficient_row(54, 40, cut_down=True)
    loop(55, EX, coefficient_rows(-14), GROUP_C)

    low = lax.broadcasted_iota(jnp.int32, (8, NZ), 0) < 4

    def swept(src, e, n, narrow):
        lines = slice(8, 48) if narrow else slice(0, EY)
        wider = narrow and src is t0

        def beside(i):
            if not wider:
                return up_y(rows[i]), down_y(rows[i])
            t = src[e - 1 + i]
            return up_y(t)[8:48], down_y(t)[8:48]

        rows = [src[e - 1 + i, lines, :] for i in range(n + 2)]
        out = []
        for i in range(n):
            t = rows[i + 1]
            above, below = beside(i + 1)
            a = t0[e + i, lines, :] + cxp[e + i, lines, :] * rows[i + 2]
            b = cyp[e + i, lines, :] * above + cym[e + i, lines, :] * below
            c = czp[e + i, lines, :] * up_z(t) + czm[e + i, lines, :] * down_z(t)
            out.append((a + cxm[e + i, lines, :] * rows[i]) + (b + c))
        return out

    def sweep(src, dst, ranges, narrow):
        lines = slice(8, 48) if narrow else slice(0, EY)

        def rows(e, n):
            for i, new in enumerate(swept(src, e, n, narrow)):
                dst[e + i, lines, :] = new

        for start, stop, _ in ranges:
            loop(start, stop, rows, GROUP)

    def last_sweep(src, dst, ranges, narrow):
        for start, stop, shift in ranges:

            def rows(e, n, shift=shift):
                for i, new in enumerate(swept(src, e, n, narrow)):
                    if narrow:
                        dst[e + shift + i, 8:32, :] = gather_middle(new, low)
                    else:
                        dst[e + shift + i] = gather_owned(new, low)

            loop(start, stop, rows, GROUP)

    def ranges(k, skip):
        return (
            (skip + k, 14 - k, 2),
            (14 + k, 54 - k, -6),
            (54 + k, EX - skip - k, -14),
        )

    def precondition(dst, skip, narrow):
        sweep(t0, ta, ranges(1, skip), narrow)
        sweep(ta, tb, ranges(2, skip), narrow)
        sweep(tb, ta, ranges(3, skip), narrow)
        last_sweep(ta, dst, ranges(4, skip), narrow)

    precondition(d1w, 0, False)

    def image_rows(xw, n):
        for i, new in enumerate([operator_row(sw, d1w, xw + i, 0, WY) for i in range(n)]):
            i1w[xw + i] = new

    loop(PAD - 5, PAD + CX + 5, image_rows, GROUP_I)

    for start, stop, shift in ranges(0, 5):

        def start_rows(e, n, shift=shift):
            for i in range(n):
                t0[e + i] = lay_out(i1w[e + shift + i]) * inv[e + i]

        loop(start, stop, start_rows, 10)
    precondition(ew, 5, True)

    place = lax.broadcasted_iota(jnp.int32, (24, NZ), 0)
    owned = (place >= 4) & (place < 20)

    def products(xw, sums):
        j = jnp.where(owned, operator_row(sw, ew, xw, 8, 32), 0.0)
        i1 = jnp.where(owned, i1w[xw, 8:32, :], 0.0)
        r = rw[xw, 8:32, :]

        def fold(v):
            return v[0:8] + v[8:16] + v[16:24]

        terms = (r * i1, i1 * i1, i1 * j, r * j, j * j)
        return tuple(acc + fold(t) for acc, t in zip(sums, terms))

    def product_rows(k, sums):
        for i in range(GROUP_P):
            sums = products(PAD + GROUP_P * k + i, sums)
        return sums

    zero = jnp.zeros((8, NZ), f32)
    sums = lax.fori_loop(0, CX // GROUP_P, product_rows, (zero,) * 5)
    block = jnp.zeros((1, NZ), f32)
    for k, acc in enumerate(sums):
        total = jnp.sum(jnp.sum(acc, axis=0, keepdims=True), axis=1, keepdims=True)
        block = jnp.where(lane8[0:1] == k, total, block)
    for k in range(copies):
        sums_out[k] = block
    d1_out[...] = d1w[PAD - 1 : PAD + CX + 1, 8:32, :]
    e_out[...] = ew[PAD - 1 : PAD + CX + 1, 8:32, :]
    s_out[...] = sw[PAD : PAD + CX, 8:32, :]


def krylov(copies, own, yl, yr, xl, xr):
    lane = np.arange(NZ)
    spread = jnp.asarray((lane[:, None] % 32 == lane[None, :] // 4).astype(np.float32), bf16)
    wide = pltpu.VMEM((WX, WY, NZ), f32)
    laid = pltpu.VMEM((EX, EY, NZ), f32)
    return pl.pallas_call(
        functools.partial(krylov_kernel, copies),
        out_shape=(
            jax.ShapeDtypeStruct((CX + 2, 24, NZ), f32),
            jax.ShapeDtypeStruct((CX + 2, 24, NZ), f32),
            jax.ShapeDtypeStruct((CX, 24, NZ), f32),
            jax.ShapeDtypeStruct((copies, 1, NZ), f32),
        ),
        scratch_shapes=[
            pltpu.VMEM((3, 2, WX // 2, NZ), f32),
            pltpu.VMEM((WX // 2, WY, NZ), f32),
            wide,
            wide,
            wide,
            wide,
            wide,
        ]
        + [laid] * 10,
        compiler_params=pltpu.CompilerParams(vmem_limit_bytes=48 << 20),
        name="krylov",
    )(own, yl, yr, xl, xr, spread)


def velocity_kernel(parts_ref, d1_ref, e_ref, s_ref, v_ref, pot_ref, moved_ref):
    totals = jnp.sum(parts_ref[...], axis=0)
    lane = lax.broadcasted_iota(jnp.int32, (1, NZ), 1)
    a, b, c, d, g = (
        jnp.sum(jnp.where(lane == k, totals, 0.0), axis=1, keepdims=True) for k in range(5)
    )
    ratio = c / b
    second = (d - ratio * a) / (g - ratio * c)
    first = a / b - ratio * second
    p1 = jnp.broadcast_to(first, (24, NZ))
    p2 = jnp.broadcast_to(second, (24, NZ))

    def row(i, before_here):
        before, here = before_here
        after = p1 * d1_ref[i + 2] + p2 * e_ref[i + 2]
        factor = COUPLING * s_ref[i]
        grad_x = 0.5 * (after - before)
        grad_y = 0.5 * (up_y(here) - down_y(here))
        pot_ref[i] = here[4:20]
        vx, vy = v_ref[0, i], v_ref[1, i]
        force_y = (factor * grad_x)[4:20]
        force_x = (factor * grad_y)[4:20]
        factor = factor[4:20]
        moved_ref[i, 0] = vx - force_x - factor * vx
        moved_ref[i, 1] = vy + force_y - factor * vy
        moved_ref[i, 2] = v_ref[2, i]
        return here, after

    lax.fori_loop(
        0, CX, row, (p1 * d1_ref[0] + p2 * e_ref[0], p1 * d1_ref[1] + p2 * e_ref[1])
    )


def velocity_step(parts, d1, e, cond, velocity):
    return pl.pallas_call(
        velocity_kernel,
        out_shape=(
            jax.ShapeDtypeStruct((CX, CY, NZ), f32),
            jax.ShapeDtypeStruct((CX, 3, CY, NZ), f32),
        ),
        compiler_params=pltpu.CompilerParams(vmem_limit_bytes=32 << 20),
        name="velocity_step",
    )(parts, d1, e, cond, velocity)


def diffusion_matrix(lines_count, cells_side):
    k = np.arange(lines_count) + 1
    phase = (k[:, None] * k[None, :]) % (2 * (lines_count + 1))
    sine = np.sqrt(2.0 / (lines_count + 1)) * np.sin(np.pi * phase / (lines_count + 1))
    half = np.sin(0.5 * np.pi * k / (lines_count + 1))
    gain = 2.0 / (1.0 + 8.0 * cells_side * cells_side * half * half)
    return (sine * gain) @ sine


def diffusion_kernel(high_ref, low_ref, x_ref, out_ref):
    high, low = high_ref[...], low_ref[...]
    for i in range(x_ref.shape[1]):
        for c in range(3):
            x = x_ref[:, i, c, :, :].reshape(high.shape[0], NZ)
            big = x.astype(bf16)
            small = (x - big.astype(f32)).astype(bf16)
            total = jnp.dot(high, small, preferred_element_type=f32)
            total = total + jnp.dot(low, big, preferred_element_type=f32)
            total = total + jnp.dot(high, big, preferred_element_type=f32)
            out_ref[c, i] = total - x


def diffuse(lines, cells_side):
    sources, count = lines.shape[0], lines.shape[1]
    length = sources * cells_side
    matrix = diffusion_matrix(length, cells_side).astype(np.float32)
    high = matrix.astype(bf16)
    low = (matrix - high.astype(np.float32)).astype(bf16)
    return pl.pallas_call(
        diffusion_kernel,
        out_shape=jax.ShapeDtypeStruct((3, count, length, NZ), f32),
        compiler_params=pltpu.CompilerParams(vmem_limit_bytes=32 << 20),
        name="diffuse",
    )(jnp.asarray(high), jnp.asarray(low), lines)


def per_device(right_side, class_map, conductivity_table, velocity):
    nx, ny = lax.axis_size("sx"), lax.axis_size("sy")

    def up(peers):
        return [(i, i + 1) for i in range(peers - 1)]

    def down(peers):
        return [(i + 1, i) for i in range(peers - 1)]

    own = message_of(conductivity_table, right_side, class_map)
    yl = lax.ppermute(own, "sy", up(ny))
    yr = lax.ppermute(own, "sy", down(ny))

    def strip(at, cond_at):
        parts = (own, yl, yr)
        cond = [m[CX : CX + 2, cond_at : cond_at + PAD // 2] for m in parts]
        cond = jnp.pad(jnp.stack(cond), ((0, 0), (0, 0), (0, 2), (0, 0)))
        rows = [m[at : at + REACH] for m in parts]
        return jnp.concatenate(rows + [cond.reshape(3, CY, NZ)], axis=0)

    xl = lax.ppermute(strip(CX - REACH, CX // 2 - PAD // 2), "sx", up(nx))
    xr = lax.ppermute(strip(0, 0), "sx", down(nx))
    d1, e, cond, sums = krylov(ny, own, yl, yr, xl, xr)
    sums = lax.all_to_all(sums, "sy", split_axis=0, concat_axis=0, tiled=True)
    sums = jnp.broadcast_to(jnp.sum(sums, axis=0, keepdims=True), (nx, 1, NZ))
    sums = lax.all_to_all(sums, "sx", split_axis=0, concat_axis=0, tiled=True)
    potential, moved = velocity_step(sums, d1, e, cond, velocity)
    lines = lax.all_to_all(
        moved.reshape(ny, CX // ny, 3, CY, NZ), "sy", split_axis=0, concat_axis=0, tiled=True
    )
    return potential, diffuse(lines, CY)


def solution(mesh):
    return jax.shard_map(
        per_device,
        mesh=mesh,
        in_specs=(P("sx", "sy", None), P("sx", "sy", None), P(), P(None, "sx", "sy", None)),
        out_specs=(P("sx", "sy", None), P(None, ("sx", "sy"), None, None)),
        check_vma=False,
    )
```

```python
import functools

import jax
import jax.numpy as jnp
import numpy as np
from jax import lax
from jax.experimental import pallas as pl
from jax.experimental.pallas import tpu as pltpu
from jax.sharding import PartitionSpec as P

CX, CY, NZ = 32, 16, 128
CLASSES = 8
PAD = 12
REACH = 10
WX, WY = CX + 2 * PAD, CY + 2 * PAD
EX = 68
EY = 56
AXIAL = 1.0 / 16.0
COUPLING = 0.25
GROUP, GROUP_C, GROUP_I, GROUP_P = 19, 13, 21, 16
f32 = jnp.float32
bf16 = jnp.bfloat16


def lay_out(row):
    return jnp.concatenate([row[0:16], row[8:32], row[24:40]], axis=0)


def gather_middle(row, low):
    return jnp.concatenate(
        [
            jnp.where(low, row[0:8], row[8:16]),
            row[16:24],
            jnp.where(low, row[24:32], row[32:40]),
        ],
        axis=0,
    )


def gather_owned(row, low):
    return jnp.concatenate([row[0:8], gather_middle(row[8:48], low), row[48:56]], axis=0)


def up_y(v):
    return pltpu.roll(v, v.shape[0] - 1, 0)


def down_y(v):
    return pltpu.roll(v, 1, 0)


def up_z(v):
    return pltpu.roll(v, v.shape[1] - 1, 1)


def down_z(v):
    return pltpu.roll(v, 1, 1)


def operator_row(s_ref, v_ref, xw, first, last):
    sl = slice(first, last)
    s, v = s_ref[xw, sl, :], v_ref[xw, sl, :]
    lane = lax.broadcasted_iota(jnp.int32, s.shape, 1)
    not_top, not_bottom = lane < NZ - 1, lane > 0
    total = (s + s_ref[xw + 1, sl, :]) * (v - v_ref[xw + 1, sl, :])
    total = total + (s + s_ref[xw - 1, sl, :]) * (v - v_ref[xw - 1, sl, :])
    total = total + (s + up_y(s)) * (v - up_y(v))
    total = total + (s + down_y(s)) * (v - down_y(v))
    axial = (s + jnp.where(not_top, up_z(s), 0.0)) * (v - jnp.where(not_top, up_z(v), 0.0))
    axial = axial + (s + jnp.where(not_bottom, down_z(s), 0.0)) * (
        v - jnp.where(not_bottom, down_z(v), 0.0)
    )
    return 0.5 * total + (0.5 * AXIAL) * axial


def loop(start, stop, body, group=1):
    whole = (stop - start) // group

    def step(k, carry):
        body(start + k * group, group)
        return carry

    if whole > 1:
        lax.fori_loop(0, whole, step, 0)
    elif whole == 1:
        body(start, group)
    if start + whole * group < stop:
        body(start + whole * group, stop - start - whole * group)


def message_kernel(table_ref, side_ref, class_ref, own_ref, low_ref, high_ref):
    own_ref[0:CX] = side_ref[...]
    low_ref[0:REACH] = side_ref[0:REACH]
    high_ref[0:REACH] = side_ref[CX - REACH : CX]
    half = PAD // 2
    for h in range(2):
        classes = jnp.concatenate([class_ref[:, 4 * h + m, :] for m in range(4)], axis=1)
        cond = jnp.zeros(classes.shape, f32)
        for k in range(CLASSES):
            cond = jnp.where(classes == k, table_ref[k], cond)
        own_ref[CX + h] = cond
        low_ref[REACH, 8 * h : 8 * h + 8, :] = cond[0:8]
        high_ref[REACH, 8 * h : 8 * h + half, :] = cond[CX // 2 - half : CX // 2]
        high_ref[REACH, 8 * h + half : 8 * h + 8, :] = cond[0 : 8 - half]


def message_of(table, right_side, class_map):
    vmem = pl.BlockSpec(memory_space=pltpu.VMEM)
    strip = jax.ShapeDtypeStruct((REACH + 1, CY, NZ), f32)
    return pl.pallas_call(
        message_kernel,
        in_specs=[pl.BlockSpec(memory_space=pltpu.SMEM), vmem, vmem],
        out_shape=(jax.ShapeDtypeStruct((CX + 2, CY, NZ), f32), strip, strip),
        name="message",
    )(table, right_side, class_map)


def krylov_kernel(
    copies,
    own_ref,
    yl_ref,
    yr_ref,
    ll_ref,
    lo_ref,
    lr_ref,
    rl_ref,
    ro_ref,
    rr_ref,
    spread_ref,
    d1_out,
    e_out,
    s_out,
    sums_out,
    sr,
    sa,
    sw,
    rw,
    d1w,
    i1w,
    ew,
    cxp,
    cxm,
    cyp,
    cym,
    czp,
    czm,
    inv,
    t0,
    ta,
    tb,
):
    xl, xr = (ll_ref, lo_ref, lr_ref), (rl_ref, ro_ref, rr_ref)

    half = PAD // 2
    for k, ref in enumerate((yl_ref, own_ref, yr_ref)):
        for h in range(2):
            sr[k, h, half : half + CX // 2, :] = ref[CX + h, :, :]
    for k in range(3):
        for h in range(2):
            at = slice(8 * h, 8 * h + half)
            sr[k, h, 0:half, :] = xl[k][REACH, at, :]
            sr[k, h, half + CX // 2 : WX // 2, :] = xr[k][REACH, at, :]

    sub = lax.broadcasted_iota(jnp.int32, (8, NZ), 0)
    lane8 = lax.broadcasted_iota(jnp.int32, (8, NZ), 1)
    low8 = sub < 4
    pick = lane8 // 32 == (sub // 2 + 2) % 4

    def spread_row(cx):
        def wide_row(part, h):
            return jnp.broadcast_to(sr[part, h, pl.ds(cx, 1), :], (8, NZ))

        pairs = (
            (wide_row(0, 0), wide_row(0, 1)),
            (wide_row(0, 1), wide_row(1, 0)),
            (wide_row(1, 0), wide_row(1, 1)),
            (wide_row(1, 1), wide_row(2, 0)),
            (wide_row(2, 0), wide_row(2, 1)),
        )
        for t, (a, b) in enumerate(pairs):
            sa[cx, 8 * t : 8 * t + 8, :] = jnp.where(pick, jnp.where(low8, a, b), 0.0)

    def spread_rows(cx, n):
        for i in range(n):
            spread_row(cx + i)

    loop(0, WX // 2, spread_rows, 4)
    spread = spread_ref[...]

    def spread_cells(c, _):
        rest = sa[pl.ds(7 * c, 7), :, :].reshape(7 * WY, NZ)
        out = jnp.zeros((7 * WY, NZ), f32)
        for _ in range(3):
            part = rest.astype(bf16)
            rest = rest - part.astype(f32)
            out = out + jnp.dot(part, spread, preferred_element_type=f32)
        out = out.reshape(7, WY, NZ)
        for k in range(7):
            sw[14 * c + 2 * k, :, :] = out[k]
            sw[14 * c + 2 * k + 1, :, :] = out[k]

    loop(0, 4, spread_cells)

    rw[PAD : PAD + CX, 0:PAD, :] = yl_ref[0:CX, CY - PAD : CY, :]
    rw[PAD : PAD + CX, PAD : PAD + CY, :] = own_ref[0:CX, :, :]
    rw[PAD : PAD + CX, PAD + CY : WY, :] = yr_ref[0:CX, 0:PAD, :]
    for refs, at in ((xl, PAD - REACH), (xr, PAD + CX)):
        rw[at : at + REACH, 0:PAD, :] = refs[0][0:REACH, CY - PAD : CY, :]
        rw[at : at + REACH, PAD : PAD + CY, :] = refs[1][0:REACH, :, :]
        rw[at : at + REACH, PAD + CY : WY, :] = refs[2][0:REACH, 0:PAD, :]

    def coefficient_row(e, xw, cut_up=False, cut_down=False):
        s5 = sw[xw]
        lane = lax.broadcasted_iota(jnp.int32, (WY, NZ), 1)
        place = lax.broadcasted_iota(jnp.int32, (EY, NZ), 0)
        zp = AXIAL * (s5 + jnp.where(lane < NZ - 1, up_z(s5), 0.0))
        zm = AXIAL * (s5 + jnp.where(lane > 0, down_z(s5), 0.0))
        axial = lay_out(zp + zm)
        s = lay_out(s5)
        yp = s + jnp.where((place == 15) | (place == 39), 0.0, lay_out(up_y(s5)))
        ym = s + jnp.where((place == 16) | (place == 40), 0.0, lay_out(down_y(s5)))
        xp = s if cut_up else s + lay_out(sw[xw + 1])
        xm = s if cut_down else s + lay_out(sw[xw - 1])
        inverse = jnp.where(s > 0.0, 1.0 / (xp + xm + yp + ym + axial), 0.0)
        cxp[e] = xp * inverse
        cxm[e] = xm * inverse
        cyp[e] = yp * inverse
        cym[e] = ym * inverse
        czp[e] = lay_out(jnp.where(lane < NZ - 1, zp, 0.0)) * inverse
        czm[e] = lay_out(jnp.where(lane > 0, zm, 0.0)) * inverse
        inverse = inverse + inverse
        inv[e] = inverse
        t0[e] = lay_out(rw[xw]) * inverse

    def coefficient_rows(shift):
        def rows(e, n):
            for i in range(n):
                coefficient_row(e + i, e + i + shift)

        return rows

    loop(0, 13, coefficient_rows(2), GROUP_C)
    coefficient_row(13, 15, cut_up=True)
    coefficient_row(14, 8, cut_down=True)
    loop(15, 53, coefficient_rows(-6), GROUP_C)
    coefficient_row(53, 47, cut_up=True)
    coefficient_row(54, 40, cut_down=True)
    loop(55, EX, coefficient_rows(-14), GROUP_C)

    low = lax.broadcasted_iota(jnp.int32, (8, NZ), 0) < 4

    def swept(src, e, n, narrow):
        lines = slice(8, 48) if narrow else slice(0, EY)
        wider = narrow and src is t0

        def beside(i):
            if not wider:
                return up_y(rows[i]), down_y(rows[i])
            t = src[e - 1 + i]
            return up_y(t)[8:48], down_y(t)[8:48]

        rows = [src[e - 1 + i, lines, :] for i in range(n + 2)]
        out = []
        for i in range(n):
            t = rows[i + 1]
            above, below = beside(i + 1)
            a = t0[e + i, lines, :] + cxp[e + i, lines, :] * rows[i + 2]
            b = cyp[e + i, lines, :] * above + cym[e + i, lines, :] * below
            c = czp[e + i, lines, :] * up_z(t) + czm[e + i, lines, :] * down_z(t)
            out.append((a + cxm[e + i, lines, :] * rows[i]) + (b + c))
        return out

    def sweep(src, dst, ranges, narrow):
        lines = slice(8, 48) if narrow else slice(0, EY)

        def rows(e, n):
            for i, new in enumerate(swept(src, e, n, narrow)):
                dst[e + i, lines, :] = new

        for start, stop, _ in ranges:
            loop(start, stop, rows, GROUP)

    def last_sweep(src, dst, ranges, narrow):
        for start, stop, shift in ranges:

            def rows(e, n, shift=shift):
                for i, new in enumerate(swept(src, e, n, narrow)):
                    if narrow:
                        dst[e + shift + i, 8:32, :] = gather_middle(new, low)
                    else:
                        dst[e + shift + i] = gather_owned(new, low)

            loop(start, stop, rows, GROUP)

    def ranges(k, skip):
        return (
            (skip + k, 14 - k, 2),
            (14 + k, 54 - k, -6),
            (54 + k, EX - skip - k, -14),
        )

    def precondition(dst, skip, narrow):
        sweep(t0, ta, ranges(1, skip), narrow)
        sweep(ta, tb, ranges(2, skip), narrow)
        sweep(tb, ta, ranges(3, skip), narrow)
        last_sweep(ta, dst, ranges(4, skip), narrow)

    precondition(d1w, 0, False)

    def image_rows(xw, n):
        for i, new in enumerate([operator_row(sw, d1w, xw + i, 0, WY) for i in range(n)]):
            i1w[xw + i] = new

    loop(PAD - 5, PAD + CX + 5, image_rows, GROUP_I)

    for start, stop, shift in ranges(0, 5):

        def start_rows(e, n, shift=shift):
            for i in range(n):
                t0[e + i] = lay_out(i1w[e + shift + i]) * inv[e + i]

        loop(start, stop, start_rows, 10)
    precondition(ew, 5, True)

    place = lax.broadcasted_iota(jnp.int32, (24, NZ), 0)
    owned = (place >= 4) & (place < 20)

    def products(xw, sums):
        j = jnp.where(owned, operator_row(sw, ew, xw, 8, 32), 0.0)
        i1 = jnp.where(owned, i1w[xw, 8:32, :], 0.0)
        r = rw[xw, 8:32, :]

        def fold(v):
            return v[0:8] + v[8:16] + v[16:24]

        terms = (r * i1, i1 * i1, i1 * j, r * j, j * j)
        return tuple(acc + fold(t) for acc, t in zip(sums, terms))

    def product_rows(k, sums):
        for i in range(GROUP_P):
            sums = products(PAD + GROUP_P * k + i, sums)
        return sums

    zero = jnp.zeros((8, NZ), f32)
    sums = lax.fori_loop(0, CX // GROUP_P, product_rows, (zero,) * 5)
    block = jnp.zeros((1, NZ), f32)
    for k, acc in enumerate(sums):
        total = jnp.sum(jnp.sum(acc, axis=0, keepdims=True), axis=1, keepdims=True)
        block = jnp.where(lane8[0:1] == k, total, block)
    for k in range(copies):
        sums_out[k] = block
    d1_out[...] = d1w[PAD - 1 : PAD + CX + 1, 8:32, :]
    e_out[...] = ew[PAD - 1 : PAD + CX + 1, 8:32, :]
    s_out[...] = sw[PAD : PAD + CX, 8:32, :]


def krylov(copies, own, yl, yr, strips):
    lane = np.arange(NZ)
    spread = jnp.asarray((lane[:, None] % 32 == lane[None, :] // 4).astype(np.float32), bf16)
    wide = pltpu.VMEM((WX, WY, NZ), f32)
    laid = pltpu.VMEM((EX, EY, NZ), f32)
    return pl.pallas_call(
        functools.partial(krylov_kernel, copies),
        out_shape=(
            jax.ShapeDtypeStruct((CX + 2, 24, NZ), f32),
            jax.ShapeDtypeStruct((CX + 2, 24, NZ), f32),
            jax.ShapeDtypeStruct((CX, 24, NZ), f32),
            jax.ShapeDtypeStruct((copies, 1, NZ), f32),
        ),
        scratch_shapes=[
            pltpu.VMEM((3, 2, WX // 2, NZ), f32),
            pltpu.VMEM((WX // 2, WY, NZ), f32),
            wide,
            wide,
            wide,
            wide,
            wide,
        ]
        + [laid] * 10,
        compiler_params=pltpu.CompilerParams(vmem_limit_bytes=48 << 20),
        name="krylov",
    )(own, yl, yr, *strips, spread)


def velocity_kernel(parts_ref, d1_ref, e_ref, s_ref, v_ref, pot_ref, moved_ref):
    totals = jnp.sum(parts_ref[...], axis=0)
    lane = lax.broadcasted_iota(jnp.int32, (1, NZ), 1)
    a, b, c, d, g = (
        jnp.sum(jnp.where(lane == k, totals, 0.0), axis=1, keepdims=True) for k in range(5)
    )
    ratio = c / b
    second = (d - ratio * a) / (g - ratio * c)
    first = a / b - ratio * second
    p1 = jnp.broadcast_to(first, (24, NZ))
    p2 = jnp.broadcast_to(second, (24, NZ))

    def row(i, before_here):
        before, here = before_here
        after = p1 * d1_ref[i + 2] + p2 * e_ref[i + 2]
        factor = COUPLING * s_ref[i]
        grad_x = 0.5 * (after - before)
        grad_y = 0.5 * (up_y(here) - down_y(here))
        pot_ref[i] = here[4:20]
        vx, vy = v_ref[0, i], v_ref[1, i]
        force_y = (factor * grad_x)[4:20]
        force_x = (factor * grad_y)[4:20]
        factor = factor[4:20]
        moved_ref[i, 0] = vx - force_x - factor * vx
        moved_ref[i, 1] = vy + force_y - factor * vy
        moved_ref[i, 2] = v_ref[2, i]
        return here, after

    lax.fori_loop(
        0, CX, row, (p1 * d1_ref[0] + p2 * e_ref[0], p1 * d1_ref[1] + p2 * e_ref[1])
    )


def velocity_step(parts, d1, e, cond, velocity):
    return pl.pallas_call(
        velocity_kernel,
        out_shape=(
            jax.ShapeDtypeStruct((CX, CY, NZ), f32),
            jax.ShapeDtypeStruct((CX, 3, CY, NZ), f32),
        ),
        compiler_params=pltpu.CompilerParams(vmem_limit_bytes=32 << 20),
        name="velocity_step",
    )(parts, d1, e, cond, velocity)


def diffusion_matrix(lines_count, cells_side):
    k = np.arange(lines_count) + 1
    phase = (k[:, None] * k[None, :]) % (2 * (lines_count + 1))
    sine = np.sqrt(2.0 / (lines_count + 1)) * np.sin(np.pi * phase / (lines_count + 1))
    half = np.sin(0.5 * np.pi * k / (lines_count + 1))
    gain = 2.0 / (1.0 + 8.0 * cells_side * cells_side * half * half)
    return (sine * gain) @ sine


def diffusion_kernel(high_ref, low_ref, x_ref, out_ref):
    high, low = high_ref[...], low_ref[...]
    for i in range(x_ref.shape[1]):
        for c in range(3):
            x = x_ref[:, i, c, :, :].reshape(high.shape[0], NZ)
            big = x.astype(bf16)
            small = (x - big.astype(f32)).astype(bf16)
            total = jnp.dot(high, small, preferred_element_type=f32)
            total = total + jnp.dot(low, big, preferred_element_type=f32)
            total = total + jnp.dot(high, big, preferred_element_type=f32)
            out_ref[c, i] = total - x


def diffuse(lines, cells_side):
    sources, count = lines.shape[0], lines.shape[1]
    length = sources * cells_side
    matrix = diffusion_matrix(length, cells_side).astype(np.float32)
    high = matrix.astype(bf16)
    low = (matrix - high.astype(np.float32)).astype(bf16)
    return pl.pallas_call(
        diffusion_kernel,
        out_shape=jax.ShapeDtypeStruct((3, count, length, NZ), f32),
        compiler_params=pltpu.CompilerParams(vmem_limit_bytes=32 << 20),
        name="diffuse",
    )(jnp.asarray(high), jnp.asarray(low), lines)


def per_device(right_side, class_map, conductivity_table, velocity):
    nx, ny = lax.axis_size("sx"), lax.axis_size("sy")

    def shifted(message, along_x, along_y):
        moves = [
            (p * ny + q, (p + along_x) * ny + q + along_y)
            for p in range(nx)
            for q in range(ny)
            if 0 <= p + along_x < nx and 0 <= q + along_y < ny
        ]
        return lax.ppermute(message, ("sx", "sy"), moves)

    own, low, high = message_of(conductivity_table, right_side, class_map)
    yl = shifted(own, 0, 1)
    yr = shifted(own, 0, -1)
    strips = [shifted(high, 1, along_y) for along_y in (1, 0, -1)]
    strips += [shifted(low, -1, along_y) for along_y in (1, 0, -1)]
    d1, e, cond, sums = krylov(ny, own, yl, yr, strips)
    sums = lax.all_to_all(sums, "sy", split_axis=0, concat_axis=0, tiled=True)
    sums = jnp.broadcast_to(jnp.sum(sums, axis=0, keepdims=True), (nx, 1, NZ))
    sums = lax.all_to_all(sums, "sx", split_axis=0, concat_axis=0, tiled=True)
    potential, moved = velocity_step(sums, d1, e, cond, velocity)
    lines = lax.all_to_all(
        moved.reshape(ny, CX // ny, 3, CY, NZ), "sy", split_axis=0, concat_axis=0, tiled=True
    )
    return potential, diffuse(lines, CY)


def solution(mesh):
    return jax.shard_map(
        per_device,
        mesh=mesh,
        in_specs=(P("sx", "sy", None), P("sx", "sy", None), P(), P(None, "sx", "sy", None)),
        out_specs=(P("sx", "sy", None), P(None, ("sx", "sy"), None, None)),
        check_vma=False,
    )
```

```python
import functools

import jax
import jax.numpy as jnp
import numpy as np
from jax import lax
from jax.experimental import pallas as pl
from jax.experimental.pallas import tpu as pltpu
from jax.sharding import PartitionSpec as P

CX, CY, NZ = 32, 16, 128
CLASSES = 8
PAD = 12
REACH = 10
WX, WY = CX + 2 * PAD, CY + 2 * PAD
EX = 68
EY = 56
AXIAL = 1.0 / 16.0
COUPLING = 0.25
GROUP, GROUP_C, GROUP_I, GROUP_P = 19, 13, 21, 16
f32 = jnp.float32
bf16 = jnp.bfloat16


def lay_out(row):
    return jnp.concatenate([row[0:16], row[8:32], row[24:40]], axis=0)


def gather_middle(row, low):
    return jnp.concatenate(
        [
            jnp.where(low, row[0:8], row[8:16]),
            row[16:24],
            jnp.where(low, row[24:32], row[32:40]),
        ],
        axis=0,
    )


def gather_owned(row, low):
    return jnp.concatenate([row[0:8], gather_middle(row[8:48], low), row[48:56]], axis=0)


def up_y(v):
    return pltpu.roll(v, v.shape[0] - 1, 0)


def down_y(v):
    return pltpu.roll(v, 1, 0)


def up_z(v):
    return pltpu.roll(v, v.shape[1] - 1, 1)


def down_z(v):
    return pltpu.roll(v, 1, 1)


def operator_row(s_ref, v_ref, xw, first, last):
    sl = slice(first, last)
    s, v = s_ref[xw, sl, :], v_ref[xw, sl, :]
    lane = lax.broadcasted_iota(jnp.int32, s.shape, 1)
    not_top, not_bottom = lane < NZ - 1, lane > 0
    total = (s + s_ref[xw + 1, sl, :]) * (v - v_ref[xw + 1, sl, :])
    total = total + (s + s_ref[xw - 1, sl, :]) * (v - v_ref[xw - 1, sl, :])
    total = total + (s + up_y(s)) * (v - up_y(v))
    total = total + (s + down_y(s)) * (v - down_y(v))
    axial = (s + jnp.where(not_top, up_z(s), 0.0)) * (v - jnp.where(not_top, up_z(v), 0.0))
    axial = axial + (s + jnp.where(not_bottom, down_z(s), 0.0)) * (
        v - jnp.where(not_bottom, down_z(v), 0.0)
    )
    return 0.5 * total + (0.5 * AXIAL) * axial


def loop(start, stop, body, group=1):
    whole = (stop - start) // group

    def step(k, carry):
        body(start + k * group, group)
        return carry

    if whole > 1:
        lax.fori_loop(0, whole, step, 0)
    elif whole == 1:
        body(start, group)
    if start + whole * group < stop:
        body(start + whole * group, stop - start - whole * group)


NEAR, NEXT, COND = 32, 8, 4
ALONG_Y = NEAR + NEXT + COND


def message_kernel(table_ref, side_ref, class_ref, up_ref, down_ref, low_ref, high_ref):
    up_ref[0:CX] = side_ref[:, 8:16, :]
    down_ref[0:CX] = side_ref[:, 0:8, :]
    for x in range(CX):
        at = slice(2 * (x % 4), 2 * (x % 4) + 2)
        up_ref[NEAR + x // 4, at, :] = side_ref[x, 6:8, :]
        down_ref[NEAR + x // 4, at, :] = side_ref[x, 8:10, :]
    low_ref[0 : 2 * REACH] = side_ref[0:REACH].reshape(2 * REACH, 8, NZ)
    high_ref[0 : 2 * REACH] = side_ref[CX - REACH : CX].reshape(2 * REACH, 8, NZ)
    for h in range(2):
        classes = jnp.concatenate([class_ref[:, 4 * h + m, :] for m in range(4)], axis=1)
        cond = jnp.zeros(classes.shape, f32)
        for k in range(CLASSES):
            cond = jnp.where(classes == k, table_ref[k], cond)
        for k in range(2):
            tile = cond[8 * k : 8 * k + 8]
            up_ref[NEAR + NEXT + 2 * h + k] = tile
            down_ref[NEAR + NEXT + 2 * h + k] = tile
            (low_ref, high_ref)[k][2 * REACH + h] = tile


def message_of(table, right_side, class_map):
    vmem = pl.BlockSpec(memory_space=pltpu.VMEM)
    along_y = jax.ShapeDtypeStruct((ALONG_Y, 8, NZ), f32)
    along_x = jax.ShapeDtypeStruct((2 * REACH + 2, 8, NZ), f32)
    return pl.pallas_call(
        message_kernel,
        in_specs=[pl.BlockSpec(memory_space=pltpu.SMEM), vmem, vmem],
        out_shape=(along_y, along_y, along_x, along_x),
        name="message",
    )(table, right_side, class_map)


def krylov_kernel(
    copies,
    own_ref,
    up_ref,
    yl_ref,
    yr_ref,
    xl_ref,
    xr_ref,
    spread_ref,
    d1_out,
    e_out,
    s_out,
    sums_out,
    sr,
    sa,
    sw,
    rw,
    d1w,
    i1w,
    ew,
    cxp,
    cxm,
    cyp,
    cym,
    czp,
    czm,
    inv,
    t0,
    ta,
    tb,
):
    half = PAD // 2
    for h in range(2):
        for k, ref in enumerate((yl_ref, up_ref, yr_ref)):
            at = NEAR + NEXT + 2 * h
            sr[k, h, half : half + 8, :] = ref[at]
            sr[k, h, half + 8 : half + 16, :] = ref[at + 1]
        for k, at in enumerate((48, 20, 50)):
            sr[k, h, 0:half, :] = xl_ref[at + h, 8 - half : 8, :]
            sr[k, h, half + 16 : 2 * half + 16, :] = xr_ref[at + h, 0:half, :]

    sub = lax.broadcasted_iota(jnp.int32, (8, NZ), 0)
    lane8 = lax.broadcasted_iota(jnp.int32, (8, NZ), 1)
    low8 = sub < 4
    pick = lane8 // 32 == (sub // 2 + 2) % 4

    def spread_row(cx):
        def wide_row(part, h):
            return jnp.broadcast_to(sr[part, h, pl.ds(cx, 1), :], (8, NZ))

        pairs = (
            (wide_row(0, 0), wide_row(0, 1)),
            (wide_row(0, 1), wide_row(1, 0)),
            (wide_row(1, 0), wide_row(1, 1)),
            (wide_row(1, 1), wide_row(2, 0)),
            (wide_row(2, 0), wide_row(2, 1)),
        )
        for t, (a, b) in enumerate(pairs):
            sa[cx, 8 * t : 8 * t + 8, :] = jnp.where(pick, jnp.where(low8, a, b), 0.0)

    def spread_rows(cx, n):
        for i in range(n):
            spread_row(cx + i)

    loop(0, WX // 2, spread_rows, 4)
    spread = spread_ref[...]

    def spread_cells(c, _):
        rest = sa[pl.ds(7 * c, 7), :, :].reshape(7 * WY, NZ)
        out = jnp.zeros((7 * WY, NZ), f32)
        for _ in range(3):
            part = rest.astype(bf16)
            rest = rest - part.astype(f32)
            out = out + jnp.dot(part, spread, preferred_element_type=f32)
        out = out.reshape(7, WY, NZ)
        for k in range(7):
            sw[14 * c + 2 * k, :, :] = out[k]
            sw[14 * c + 2 * k + 1, :, :] = out[k]

    loop(0, 4, spread_cells)

    def place(at, rows, own, first, near_l, near_r, next_l, next_r):
        rw[at : at + rows, PAD : PAD + CY, :] = own
        rw[at : at + rows, PAD - 8 : PAD, :] = near_l
        rw[at : at + rows, PAD + CY : PAD + CY + 8, :] = near_r
        rw[at : at + rows, 0:2, :] = jnp.zeros((rows, 2, NZ), f32)
        rw[at : at + rows, WY - 2 : WY, :] = jnp.zeros((rows, 2, NZ), f32)
        for i in range(rows):
            x = first + i
            tile, lines = x // 4 - first // 4, slice(2 * (x % 4), 2 * (x % 4) + 2)
            for (ref, start), to in ((next_l, PAD - 10), (next_r, PAD + CY + 8)):
                rw[at + i, to : to + 2, :] = ref[start + tile, lines, :]

    place(
        PAD, CX, own_ref[...], 0, yl_ref[0:CX], yr_ref[0:CX], (yl_ref, NEAR), (yr_ref, NEAR)
    )
    for ref, at, first in ((xl_ref, PAD - REACH, CX - REACH), (xr_ref, PAD + CX, 0)):
        own = ref[0 : 2 * REACH].reshape(REACH, CY, NZ)
        near_l, near_r = ref[22:32], ref[32:42]
        place(at, REACH, own, first, near_l, near_r, (ref, 42), (ref, 45))

    def coefficient_row(e, xw, cut_up=False, cut_down=False):
        s5 = sw[xw]
        lane = lax.broadcasted_iota(jnp.int32, (WY, NZ), 1)
        place = lax.broadcasted_iota(jnp.int32, (EY, NZ), 0)
        zp = AXIAL * (s5 + jnp.where(lane < NZ - 1, up_z(s5), 0.0))
        zm = AXIAL * (s5 + jnp.where(lane > 0, down_z(s5), 0.0))
        axial = lay_out(zp + zm)
        s = lay_out(s5)
        yp = s + jnp.where((place == 15) | (place == 39), 0.0, lay_out(up_y(s5)))
        ym = s + jnp.where((place == 16) | (place == 40), 0.0, lay_out(down_y(s5)))
        xp = s if cut_up else s + lay_out(sw[xw + 1])
        xm = s if cut_down else s + lay_out(sw[xw - 1])
        inverse = jnp.where(s > 0.0, 1.0 / (xp + xm + yp + ym + axial), 0.0)
        cxp[e] = xp * inverse
        cxm[e] = xm * inverse
        cyp[e] = yp * inverse
        cym[e] = ym * inverse
        czp[e] = lay_out(jnp.where(lane < NZ - 1, zp, 0.0)) * inverse
        czm[e] = lay_out(jnp.where(lane > 0, zm, 0.0)) * inverse
        inverse = inverse + inverse
        inv[e] = inverse
        t0[e] = lay_out(rw[xw]) * inverse

    def coefficient_rows(shift):
        def rows(e, n):
            for i in range(n):
                coefficient_row(e + i, e + i + shift)

        return rows

    loop(0, 13, coefficient_rows(2), GROUP_C)
    coefficient_row(13, 15, cut_up=True)
    coefficient_row(14, 8, cut_down=True)
    loop(15, 53, coefficient_rows(-6), GROUP_C)
    coefficient_row(53, 47, cut_up=True)
    coefficient_row(54, 40, cut_down=True)
    loop(55, EX, coefficient_rows(-14), GROUP_C)

    low = lax.broadcasted_iota(jnp.int32, (8, NZ), 0) < 4

    def swept(src, e, n, narrow):
        lines = slice(8, 48) if narrow else slice(0, EY)
        wider = narrow and src is t0

        def beside(i):
            if not wider:
                return up_y(rows[i]), down_y(rows[i])
            t = src[e - 1 + i]
            return up_y(t)[8:48], down_y(t)[8:48]

        rows = [src[e - 1 + i, lines, :] for i in range(n + 2)]
        out = []
        for i in range(n):
            t = rows[i + 1]
            above, below = beside(i + 1)
            a = t0[e + i, lines, :] + cxp[e + i, lines, :] * rows[i + 2]
            b = cyp[e + i, lines, :] * above + cym[e + i, lines, :] * below
            c = czp[e + i, lines, :] * up_z(t) + czm[e + i, lines, :] * down_z(t)
            out.append((a + cxm[e + i, lines, :] * rows[i]) + (b + c))
        return out

    def sweep(src, dst, ranges, narrow):
        lines = slice(8, 48) if narrow else slice(0, EY)

        def rows(e, n):
            for i, new in enumerate(swept(src, e, n, narrow)):
                dst[e + i, lines, :] = new

        for start, stop, _ in ranges:
            loop(start, stop, rows, GROUP)

    def last_sweep(src, dst, ranges, narrow):
        for start, stop, shift in ranges:

            def rows(e, n, shift=shift):
                for i, new in enumerate(swept(src, e, n, narrow)):
                    if narrow:
                        dst[e + shift + i, 8:32, :] = gather_middle(new, low)
                    else:
                        dst[e + shift + i] = gather_owned(new, low)

            loop(start, stop, rows, GROUP)

    def ranges(k, skip):
        return (
            (skip + k, 14 - k, 2),
            (14 + k, 54 - k, -6),
            (54 + k, EX - skip - k, -14),
        )

    def precondition(dst, skip, narrow):
        sweep(t0, ta, ranges(1, skip), narrow)
        sweep(ta, tb, ranges(2, skip), narrow)
        sweep(tb, ta, ranges(3, skip), narrow)
        last_sweep(ta, dst, ranges(4, skip), narrow)

    precondition(d1w, 0, False)

    def image_rows(xw, n):
        for i, new in enumerate([operator_row(sw, d1w, xw + i, 0, WY) for i in range(n)]):
            i1w[xw + i] = new

    loop(PAD - 5, PAD + CX + 5, image_rows, GROUP_I)

    for start, stop, shift in ranges(0, 5):

        def start_rows(e, n, shift=shift):
            for i in range(n):
                t0[e + i] = lay_out(i1w[e + shift + i]) * inv[e + i]

        loop(start, stop, start_rows, 10)
    precondition(ew, 5, True)

    place = lax.broadcasted_iota(jnp.int32, (24, NZ), 0)
    owned = (place >= 4) & (place < 20)

    def products(xw, sums):
        j = jnp.where(owned, operator_row(sw, ew, xw, 8, 32), 0.0)
        i1 = jnp.where(owned, i1w[xw, 8:32, :], 0.0)
        r = rw[xw, 8:32, :]

        def fold(v):
            return v[0:8] + v[8:16] + v[16:24]

        terms = (r * i1, i1 * i1, i1 * j, r * j, j * j)
        return tuple(acc + fold(t) for acc, t in zip(sums, terms))

    def product_rows(k, sums):
        for i in range(GROUP_P):
            sums = products(PAD + GROUP_P * k + i, sums)
        return sums

    zero = jnp.zeros((8, NZ), f32)
    sums = lax.fori_loop(0, CX // GROUP_P, product_rows, (zero,) * 5)
    block = jnp.zeros((1, NZ), f32)
    for k, acc in enumerate(sums):
        total = jnp.sum(jnp.sum(acc, axis=0, keepdims=True), axis=1, keepdims=True)
        block = jnp.where(lane8[0:1] == k, total, block)
    for k in range(copies):
        sums_out[k] = block
    d1_out[...] = d1w[PAD - 1 : PAD + CX + 1, 8:32, :]
    e_out[...] = ew[PAD - 1 : PAD + CX + 1, 8:32, :]
    s_out[...] = sw[PAD : PAD + CX, 8:32, :]


def krylov(copies, own, up, yl, yr, xl, xr):
    lane = np.arange(NZ)
    spread = jnp.asarray((lane[:, None] % 32 == lane[None, :] // 4).astype(np.float32), bf16)
    wide = pltpu.VMEM((WX, WY, NZ), f32)
    laid = pltpu.VMEM((EX, EY, NZ), f32)
    return pl.pallas_call(
        functools.partial(krylov_kernel, copies),
        out_shape=(
            jax.ShapeDtypeStruct((CX + 2, 24, NZ), f32),
            jax.ShapeDtypeStruct((CX + 2, 24, NZ), f32),
            jax.ShapeDtypeStruct((CX, 24, NZ), f32),
            jax.ShapeDtypeStruct((copies, 1, NZ), f32),
        ),
        scratch_shapes=[
            pltpu.VMEM((3, 2, WX // 2, NZ), f32),
            pltpu.VMEM((WX // 2, WY, NZ), f32),
            wide,
            wide,
            wide,
            wide,
            wide,
        ]
        + [laid] * 10,
        compiler_params=pltpu.CompilerParams(vmem_limit_bytes=48 << 20),
        name="krylov",
    )(own, up, yl, yr, xl, xr, spread)


def velocity_kernel(parts_ref, d1_ref, e_ref, s_ref, v_ref, pot_ref, moved_ref):
    totals = jnp.sum(parts_ref[...], axis=0)
    lane = lax.broadcasted_iota(jnp.int32, (1, NZ), 1)
    a, b, c, d, g = (
        jnp.sum(jnp.where(lane == k, totals, 0.0), axis=1, keepdims=True) for k in range(5)
    )
    ratio = c / b
    second = (d - ratio * a) / (g - ratio * c)
    first = a / b - ratio * second
    p1 = jnp.broadcast_to(first, (24, NZ))
    p2 = jnp.broadcast_to(second, (24, NZ))

    def row(i, before_here):
        before, here = before_here
        after = p1 * d1_ref[i + 2] + p2 * e_ref[i + 2]
        factor = COUPLING * s_ref[i]
        grad_x = 0.5 * (after - before)
        grad_y = 0.5 * (up_y(here) - down_y(here))
        pot_ref[i] = here[4:20]
        vx, vy = v_ref[0, i], v_ref[1, i]
        force_y = (factor * grad_x)[4:20]
        force_x = (factor * grad_y)[4:20]
        factor = factor[4:20]
        moved_ref[i, 0] = vx - force_x - factor * vx
        moved_ref[i, 1] = vy + force_y - factor * vy
        moved_ref[i, 2] = v_ref[2, i]
        return here, after

    lax.fori_loop(
        0, CX, row, (p1 * d1_ref[0] + p2 * e_ref[0], p1 * d1_ref[1] + p2 * e_ref[1])
    )


def velocity_step(parts, d1, e, cond, velocity):
    return pl.pallas_call(
        velocity_kernel,
        out_shape=(
            jax.ShapeDtypeStruct((CX, CY, NZ), f32),
            jax.ShapeDtypeStruct((CX, 3, CY, NZ), f32),
        ),
        compiler_params=pltpu.CompilerParams(vmem_limit_bytes=32 << 20),
        name="velocity_step",
    )(parts, d1, e, cond, velocity)


def diffusion_matrix(lines_count, cells_side):
    k = np.arange(lines_count) + 1
    phase = (k[:, None] * k[None, :]) % (2 * (lines_count + 1))
    sine = np.sqrt(2.0 / (lines_count + 1)) * np.sin(np.pi * phase / (lines_count + 1))
    half = np.sin(0.5 * np.pi * k / (lines_count + 1))
    gain = 2.0 / (1.0 + 8.0 * cells_side * cells_side * half * half)
    return (sine * gain) @ sine


def diffusion_kernel(high_ref, low_ref, x_ref, out_ref):
    high, low = high_ref[...], low_ref[...]
    for i in range(x_ref.shape[1]):
        for c in range(3):
            x = x_ref[:, i, c, :, :].reshape(high.shape[0], NZ)
            big = x.astype(bf16)
            small = (x - big.astype(f32)).astype(bf16)
            total = jnp.dot(high, small, preferred_element_type=f32)
            total = total + jnp.dot(low, big, preferred_element_type=f32)
            total = total + jnp.dot(high, big, preferred_element_type=f32)
            out_ref[c, i] = total - x


def diffuse(lines, cells_side):
    sources, count = lines.shape[0], lines.shape[1]
    length = sources * cells_side
    matrix = diffusion_matrix(length, cells_side).astype(np.float32)
    high = matrix.astype(bf16)
    low = (matrix - high.astype(np.float32)).astype(bf16)
    return pl.pallas_call(
        diffusion_kernel,
        out_shape=jax.ShapeDtypeStruct((3, count, length, NZ), f32),
        compiler_params=pltpu.CompilerParams(vmem_limit_bytes=32 << 20),
        name="diffuse",
    )(jnp.asarray(high), jnp.asarray(low), lines)


def per_device(right_side, class_map, conductivity_table, velocity):
    nx, ny = lax.axis_size("sx"), lax.axis_size("sy")

    def up(peers):
        return [(i, i + 1) for i in range(peers - 1)]

    def down(peers):
        return [(i + 1, i) for i in range(peers - 1)]

    to_up, to_down, low, high = message_of(conductivity_table, right_side, class_map)
    yl = lax.ppermute(to_up, "sy", up(ny))
    yr = lax.ppermute(to_down, "sy", down(ny))

    def strip(own, at, next_at, k):
        pieces = [own]
        pieces += [m[at : at + REACH] for m in (yl, yr)]
        pieces += [m[NEAR + next_at : NEAR + next_at + 3] for m in (yl, yr)]
        for m in (yl, yr):
            pieces += [m[NEAR + NEXT + 2 * h + k :][:1] for h in range(2)]
        return jnp.concatenate(pieces, axis=0)

    xl = lax.ppermute(strip(high, CX - REACH, 5, 1), "sx", up(nx))
    xr = lax.ppermute(strip(low, 0, 0, 0), "sx", down(nx))
    d1, e, cond, sums = krylov(ny, right_side, to_up, yl, yr, xl, xr)
    sums = lax.all_to_all(sums, "sy", split_axis=0, concat_axis=0, tiled=True)
    sums = jnp.broadcast_to(jnp.sum(sums, axis=0, keepdims=True), (nx, 1, NZ))
    sums = lax.all_to_all(sums, "sx", split_axis=0, concat_axis=0, tiled=True)
    potential, moved = velocity_step(sums, d1, e, cond, velocity)
    lines = lax.all_to_all(
        moved.reshape(ny, CX // ny, 3, CY, NZ), "sy", split_axis=0, concat_axis=0, tiled=True
    )
    return potential, diffuse(lines, CY)


def solution(mesh):
    return jax.shard_map(
        per_device,
        mesh=mesh,
        in_specs=(P("sx", "sy", None), P("sx", "sy", None), P(), P(None, "sx", "sy", None)),
        out_specs=(P("sx", "sy", None), P(None, ("sx", "sy"), None, None)),
        check_vma=False,
    )
```

```python
import functools

import jax
import jax.numpy as jnp
import numpy as np
from jax import lax
from jax.experimental import pallas as pl
from jax.experimental.pallas import tpu as pltpu
from jax.sharding import PartitionSpec as P

CX, CY, NZ = 32, 16, 128
CLASSES = 8
PAD = 12
REACH = 10
WX, WY = CX + 2 * PAD, CY + 2 * PAD
EX = 68
EY = 56
AXIAL = 1.0 / 16.0
COUPLING = 0.25
GROUP, GROUP_C, GROUP_I, GROUP_P = 19, 13, 21, 16
f32 = jnp.float32
bf16 = jnp.bfloat16


def lay_out(row):
    return jnp.concatenate([row[0:16], row[8:32], row[24:40]], axis=0)


def gather_middle(row, low):
    return jnp.concatenate(
        [
            jnp.where(low, row[0:8], row[8:16]),
            row[16:24],
            jnp.where(low, row[24:32], row[32:40]),
        ],
        axis=0,
    )


def gather_owned(row, low):
    return jnp.concatenate([row[0:8], gather_middle(row[8:48], low), row[48:56]], axis=0)


def up_y(v):
    return pltpu.roll(v, v.shape[0] - 1, 0)


def down_y(v):
    return pltpu.roll(v, 1, 0)


def up_z(v):
    return pltpu.roll(v, v.shape[1] - 1, 1)


def down_z(v):
    return pltpu.roll(v, 1, 1)


def operator_row(s_ref, v_ref, xw, first, last):
    sl = slice(first, last)
    s, v = s_ref[xw, sl, :], v_ref[xw, sl, :]
    lane = lax.broadcasted_iota(jnp.int32, s.shape, 1)
    not_top, not_bottom = lane < NZ - 1, lane > 0
    total = (s + s_ref[xw + 1, sl, :]) * (v - v_ref[xw + 1, sl, :])
    total = total + (s + s_ref[xw - 1, sl, :]) * (v - v_ref[xw - 1, sl, :])
    total = total + (s + up_y(s)) * (v - up_y(v))
    total = total + (s + down_y(s)) * (v - down_y(v))
    axial = (s + jnp.where(not_top, up_z(s), 0.0)) * (v - jnp.where(not_top, up_z(v), 0.0))
    axial = axial + (s + jnp.where(not_bottom, down_z(s), 0.0)) * (
        v - jnp.where(not_bottom, down_z(v), 0.0)
    )
    return 0.5 * total + (0.5 * AXIAL) * axial


def loop(start, stop, body, group=1):
    whole = (stop - start) // group

    def step(k, carry):
        body(start + k * group, group)
        return carry

    if whole > 1:
        lax.fori_loop(0, whole, step, 0)
    elif whole == 1:
        body(start, group)
    if start + whole * group < stop:
        body(start + whole * group, stop - start - whole * group)


NEAR, NEXT, COND = 32, 8, 4
ALONG_Y = NEAR + NEXT + COND


def message_kernel(
    odd_ref, table_ref, side_ref, class_ref, first_ref, second_ref, low_ref, high_ref
):
    def sides(up_ref, down_ref):
        up_ref[0:CX] = side_ref[:, 8:16, :]
        down_ref[0:CX] = side_ref[:, 0:8, :]
        for x in range(CX):
            at = slice(2 * (x % 4), 2 * (x % 4) + 2)
            up_ref[NEAR + x // 4, at, :] = side_ref[x, 6:8, :]
            down_ref[NEAR + x // 4, at, :] = side_ref[x, 8:10, :]

    @pl.when(odd_ref[0] == 0)
    def _():
        sides(first_ref, second_ref)

    @pl.when(odd_ref[0] == 1)
    def _():
        sides(second_ref, first_ref)

    low_ref[0 : 2 * REACH] = side_ref[0:REACH].reshape(2 * REACH, 8, NZ)
    high_ref[0 : 2 * REACH] = side_ref[CX - REACH : CX].reshape(2 * REACH, 8, NZ)
    for h in range(2):
        classes = jnp.concatenate([class_ref[:, 4 * h + m, :] for m in range(4)], axis=1)
        cond = jnp.zeros(classes.shape, f32)
        for k in range(CLASSES):
            cond = jnp.where(classes == k, table_ref[k], cond)
        for k in range(2):
            tile = cond[8 * k : 8 * k + 8]
            first_ref[NEAR + NEXT + 2 * h + k] = tile
            second_ref[NEAR + NEXT + 2 * h + k] = tile
            (low_ref, high_ref)[k][2 * REACH + h] = tile


def message_of(odd, table, right_side, class_map):
    vmem = pl.BlockSpec(memory_space=pltpu.VMEM)
    smem = pl.BlockSpec(memory_space=pltpu.SMEM)
    along_y = jax.ShapeDtypeStruct((ALONG_Y, 8, NZ), f32)
    along_x = jax.ShapeDtypeStruct((2 * REACH + 2, 8, NZ), f32)
    return pl.pallas_call(
        message_kernel,
        in_specs=[smem, smem, vmem, vmem],
        out_shape=(along_y, along_y, along_x, along_x),
        name="message",
    )(odd, table, right_side, class_map)


def krylov_kernel(
    copies,
    odd_ref,
    own_ref,
    mine_ref,
    ya_ref,
    yb_ref,
    xl_ref,
    xr_ref,
    spread_ref,
    d1_out,
    e_out,
    s_out,
    sums_out,
    sr,
    sa,
    sw,
    rw,
    d1w,
    i1w,
    ew,
    cxp,
    cxm,
    cyp,
    cym,
    czp,
    czm,
    inv,
    t0,
    ta,
    tb,
):
    half = PAD // 2

    def place(at, rows, own, first, near_l, near_r, next_l, next_r):
        rw[at : at + rows, PAD : PAD + CY, :] = own
        rw[at : at + rows, PAD - 8 : PAD, :] = near_l
        rw[at : at + rows, PAD + CY : PAD + CY + 8, :] = near_r
        rw[at : at + rows, 0:2, :] = jnp.zeros((rows, 2, NZ), f32)
        rw[at : at + rows, WY - 2 : WY, :] = jnp.zeros((rows, 2, NZ), f32)
        for i in range(rows):
            x = first + i
            tile, lines = x // 4 - first // 4, slice(2 * (x % 4), 2 * (x % 4) + 2)
            for (ref, start), to in ((next_l, PAD - 10), (next_r, PAD + CY + 8)):
                rw[at + i, to : to + 2, :] = ref[start + tile, lines, :]

    def unpack(yl_ref, yr_ref, l, r):
        for h in range(2):
            for k, ref in enumerate((yl_ref, mine_ref, yr_ref)):
                at = NEAR + NEXT + 2 * h
                sr[k, h, half : half + 8, :] = ref[at]
                sr[k, h, half + 8 : half + 16, :] = ref[at + 1]
            for k, at in enumerate((48 + 2 * l, 20, 48 + 2 * r)):
                sr[k, h, 0:half, :] = xl_ref[at + h, 8 - half : 8, :]
                sr[k, h, half + 16 : 2 * half + 16, :] = xr_ref[at + h, 0:half, :]
        next_y = (yl_ref, NEAR), (yr_ref, NEAR)
        place(PAD, CX, own_ref[...], 0, yl_ref[0:CX], yr_ref[0:CX], *next_y)
        for ref, at, first in ((xl_ref, PAD - REACH, CX - REACH), (xr_ref, PAD + CX, 0)):
            own = ref[0 : 2 * REACH].reshape(REACH, CY, NZ)
            near_l, near_r = (ref[22 + 10 * k : 32 + 10 * k] for k in (l, r))
            place(at, REACH, own, first, near_l, near_r, (ref, 42 + 3 * l), (ref, 42 + 3 * r))

    @pl.when(odd_ref[0] == 0)
    def _():
        unpack(yb_ref, ya_ref, 1, 0)

    @pl.when(odd_ref[0] == 1)
    def _():
        unpack(ya_ref, yb_ref, 0, 1)

    sub = lax.broadcasted_iota(jnp.int32, (8, NZ), 0)
    lane8 = lax.broadcasted_iota(jnp.int32, (8, NZ), 1)
    low8 = sub < 4
    pick = lane8 // 32 == (sub // 2 + 2) % 4

    def spread_row(cx):
        def wide_row(part, h):
            return jnp.broadcast_to(sr[part, h, pl.ds(cx, 1), :], (8, NZ))

        pairs = (
            (wide_row(0, 0), wide_row(0, 1)),
            (wide_row(0, 1), wide_row(1, 0)),
            (wide_row(1, 0), wide_row(1, 1)),
            (wide_row(1, 1), wide_row(2, 0)),
            (wide_row(2, 0), wide_row(2, 1)),
        )
        for t, (a, b) in enumerate(pairs):
            sa[cx, 8 * t : 8 * t + 8, :] = jnp.where(pick, jnp.where(low8, a, b), 0.0)

    def spread_rows(cx, n):
        for i in range(n):
            spread_row(cx + i)

    loop(0, WX // 2, spread_rows, 4)
    spread = spread_ref[...]

    def spread_cells(c, _):
        rest = sa[pl.ds(7 * c, 7), :, :].reshape(7 * WY, NZ)
        out = jnp.zeros((7 * WY, NZ), f32)
        for _ in range(3):
            part = rest.astype(bf16)
            rest = rest - part.astype(f32)
            out = out + jnp.dot(part, spread, preferred_element_type=f32)
        out = out.reshape(7, WY, NZ)
        for k in range(7):
            sw[14 * c + 2 * k, :, :] = out[k]
            sw[14 * c + 2 * k + 1, :, :] = out[k]

    loop(0, 4, spread_cells)

    def coefficient_row(e, xw, cut_up=False, cut_down=False):
        s5 = sw[xw]
        lane = lax.broadcasted_iota(jnp.int32, (WY, NZ), 1)
        place = lax.broadcasted_iota(jnp.int32, (EY, NZ), 0)
        zp = AXIAL * (s5 + jnp.where(lane < NZ - 1, up_z(s5), 0.0))
        zm = AXIAL * (s5 + jnp.where(lane > 0, down_z(s5), 0.0))
        axial = lay_out(zp + zm)
        s = lay_out(s5)
        yp = s + jnp.where((place == 15) | (place == 39), 0.0, lay_out(up_y(s5)))
        ym = s + jnp.where((place == 16) | (place == 40), 0.0, lay_out(down_y(s5)))
        xp = s if cut_up else s + lay_out(sw[xw + 1])
        xm = s if cut_down else s + lay_out(sw[xw - 1])
        inverse = jnp.where(s > 0.0, 1.0 / (xp + xm + yp + ym + axial), 0.0)
        cxp[e] = xp * inverse
        cxm[e] = xm * inverse
        cyp[e] = yp * inverse
        cym[e] = ym * inverse
        czp[e] = lay_out(jnp.where(lane < NZ - 1, zp, 0.0)) * inverse
        czm[e] = lay_out(jnp.where(lane > 0, zm, 0.0)) * inverse
        inverse = inverse + inverse
        inv[e] = inverse
        t0[e] = lay_out(rw[xw]) * inverse

    def coefficient_rows(shift):
        def rows(e, n):
            for i in range(n):
                coefficient_row(e + i, e + i + shift)

        return rows

    loop(0, 13, coefficient_rows(2), GROUP_C)
    coefficient_row(13, 15, cut_up=True)
    coefficient_row(14, 8, cut_down=True)
    loop(15, 53, coefficient_rows(-6), GROUP_C)
    coefficient_row(53, 47, cut_up=True)
    coefficient_row(54, 40, cut_down=True)
    loop(55, EX, coefficient_rows(-14), GROUP_C)

    low = lax.broadcasted_iota(jnp.int32, (8, NZ), 0) < 4

    def swept(src, e, n, narrow):
        lines = slice(8, 48) if narrow else slice(0, EY)
        wider = narrow and src is t0

        def beside(i):
            if not wider:
                return up_y(rows[i]), down_y(rows[i])
            t = src[e - 1 + i]
            return up_y(t)[8:48], down_y(t)[8:48]

        rows = [src[e - 1 + i, lines, :] for i in range(n + 2)]
        out = []
        for i in range(n):
            t = rows[i + 1]
            above, below = beside(i + 1)
            a = t0[e + i, lines, :] + cxp[e + i, lines, :] * rows[i + 2]
            b = cyp[e + i, lines, :] * above + cym[e + i, lines, :] * below
            c = czp[e + i, lines, :] * up_z(t) + czm[e + i, lines, :] * down_z(t)
            out.append((a + cxm[e + i, lines, :] * rows[i]) + (b + c))
        return out

    def sweep(src, dst, ranges, narrow):
        lines = slice(8, 48) if narrow else slice(0, EY)

        def rows(e, n):
            for i, new in enumerate(swept(src, e, n, narrow)):
                dst[e + i, lines, :] = new

        for start, stop, _ in ranges:
            loop(start, stop, rows, GROUP)

    def last_sweep(src, dst, ranges, narrow):
        for start, stop, shift in ranges:

            def rows(e, n, shift=shift):
                for i, new in enumerate(swept(src, e, n, narrow)):
                    if narrow:
                        dst[e + shift + i, 8:32, :] = gather_middle(new, low)
                    else:
                        dst[e + shift + i] = gather_owned(new, low)

            loop(start, stop, rows, GROUP)

    def ranges(k, skip):
        return (
            (skip + k, 14 - k, 2),
            (14 + k, 54 - k, -6),
            (54 + k, EX - skip - k, -14),
        )

    def precondition(dst, skip, narrow):
        sweep(t0, ta, ranges(1, skip), narrow)
        sweep(ta, tb, ranges(2, skip), narrow)
        sweep(tb, ta, ranges(3, skip), narrow)
        last_sweep(ta, dst, ranges(4, skip), narrow)

    precondition(d1w, 0, False)

    def image_rows(xw, n):
        for i, new in enumerate([operator_row(sw, d1w, xw + i, 0, WY) for i in range(n)]):
            i1w[xw + i] = new

    loop(PAD - 5, PAD + CX + 5, image_rows, GROUP_I)

    for start, stop, shift in ranges(0, 5):

        def start_rows(e, n, shift=shift):
            for i in range(n):
                t0[e + i] = lay_out(i1w[e + shift + i]) * inv[e + i]

        loop(start, stop, start_rows, 10)
    precondition(ew, 5, True)

    place = lax.broadcasted_iota(jnp.int32, (24, NZ), 0)
    owned = (place >= 4) & (place < 20)

    def products(xw, sums):
        j = jnp.where(owned, operator_row(sw, ew, xw, 8, 32), 0.0)
        i1 = jnp.where(owned, i1w[xw, 8:32, :], 0.0)
        r = rw[xw, 8:32, :]

        def fold(v):
            return v[0:8] + v[8:16] + v[16:24]

        terms = (r * i1, i1 * i1, i1 * j, r * j, j * j)
        return tuple(acc + fold(t) for acc, t in zip(sums, terms))

    def product_rows(k, sums):
        for i in range(GROUP_P):
            sums = products(PAD + GROUP_P * k + i, sums)
        return sums

    zero = jnp.zeros((8, NZ), f32)
    sums = lax.fori_loop(0, CX // GROUP_P, product_rows, (zero,) * 5)
    block = jnp.zeros((1, NZ), f32)
    for k, acc in enumerate(sums):
        total = jnp.sum(jnp.sum(acc, axis=0, keepdims=True), axis=1, keepdims=True)
        block = jnp.where(lane8[0:1] == k, total, block)
    for k in range(copies):
        sums_out[k] = block
    d1_out[...] = d1w[PAD - 1 : PAD + CX + 1, 8:32, :]
    e_out[...] = ew[PAD - 1 : PAD + CX + 1, 8:32, :]
    s_out[...] = sw[PAD : PAD + CX, 8:32, :]


def krylov(copies, odd, own, mine, ya, yb, xl, xr):
    smem, vmem = (pl.BlockSpec(memory_space=m) for m in (pltpu.SMEM, pltpu.VMEM))
    lane = np.arange(NZ)
    spread = jnp.asarray((lane[:, None] % 32 == lane[None, :] // 4).astype(np.float32), bf16)
    wide = pltpu.VMEM((WX, WY, NZ), f32)
    laid = pltpu.VMEM((EX, EY, NZ), f32)
    return pl.pallas_call(
        functools.partial(krylov_kernel, copies),
        in_specs=[smem] + [vmem] * 7,
        out_shape=(
            jax.ShapeDtypeStruct((CX + 2, 24, NZ), f32),
            jax.ShapeDtypeStruct((CX + 2, 24, NZ), f32),
            jax.ShapeDtypeStruct((CX, 24, NZ), f32),
            jax.ShapeDtypeStruct((copies, 1, NZ), f32),
        ),
        scratch_shapes=[
            pltpu.VMEM((3, 2, WX // 2, NZ), f32),
            pltpu.VMEM((WX // 2, WY, NZ), f32),
            wide,
            wide,
            wide,
            wide,
            wide,
        ]
        + [laid] * 10,
        compiler_params=pltpu.CompilerParams(vmem_limit_bytes=48 << 20),
        name="krylov",
    )(odd, own, mine, ya, yb, xl, xr, spread)


def velocity_kernel(parts_ref, d1_ref, e_ref, s_ref, v_ref, pot_ref, moved_ref):
    totals = jnp.sum(parts_ref[...], axis=0)
    lane = lax.broadcasted_iota(jnp.int32, (1, NZ), 1)
    a, b, c, d, g = (
        jnp.sum(jnp.where(lane == k, totals, 0.0), axis=1, keepdims=True) for k in range(5)
    )
    ratio = c / b
    second = (d - ratio * a) / (g - ratio * c)
    first = a / b - ratio * second
    p1 = jnp.broadcast_to(first, (24, NZ))
    p2 = jnp.broadcast_to(second, (24, NZ))

    def row(i, before_here):
        before, here = before_here
        after = p1 * d1_ref[i + 2] + p2 * e_ref[i + 2]
        factor = COUPLING * s_ref[i]
        grad_x = 0.5 * (after - before)
        grad_y = 0.5 * (up_y(here) - down_y(here))
        pot_ref[i] = here[4:20]
        vx, vy = v_ref[0, i], v_ref[1, i]
        force_y = (factor * grad_x)[4:20]
        force_x = (factor * grad_y)[4:20]
        factor = factor[4:20]
        moved_ref[i, 0] = vx - force_x - factor * vx
        moved_ref[i, 1] = vy + force_y - factor * vy
        moved_ref[i, 2] = v_ref[2, i]
        return here, after

    lax.fori_loop(
        0, CX, row, (p1 * d1_ref[0] + p2 * e_ref[0], p1 * d1_ref[1] + p2 * e_ref[1])
    )


def velocity_step(parts, d1, e, cond, velocity):
    return pl.pallas_call(
        velocity_kernel,
        out_shape=(
            jax.ShapeDtypeStruct((CX, CY, NZ), f32),
            jax.ShapeDtypeStruct((CX, 3, CY, NZ), f32),
        ),
        compiler_params=pltpu.CompilerParams(vmem_limit_bytes=32 << 20),
        name="velocity_step",
    )(parts, d1, e, cond, velocity)


def diffusion_matrix(lines_count, cells_side):
    k = np.arange(lines_count) + 1
    phase = (k[:, None] * k[None, :]) % (2 * (lines_count + 1))
    sine = np.sqrt(2.0 / (lines_count + 1)) * np.sin(np.pi * phase / (lines_count + 1))
    half = np.sin(0.5 * np.pi * k / (lines_count + 1))
    gain = 2.0 / (1.0 + 8.0 * cells_side * cells_side * half * half)
    return (sine * gain) @ sine


def diffusion_kernel(high_ref, low_ref, x_ref, out_ref):
    high, low = high_ref[...], low_ref[...]
    for i in range(x_ref.shape[1]):
        for c in range(3):
            x = x_ref[:, i, c, :, :].reshape(high.shape[0], NZ)
            big = x.astype(bf16)
            small = (x - big.astype(f32)).astype(bf16)
            total = jnp.dot(high, small, preferred_element_type=f32)
            total = total + jnp.dot(low, big, preferred_element_type=f32)
            total = total + jnp.dot(high, big, preferred_element_type=f32)
            out_ref[c, i] = total - x


def diffuse(lines, cells_side):
    sources, count = lines.shape[0], lines.shape[1]
    length = sources * cells_side
    matrix = diffusion_matrix(length, cells_side).astype(np.float32)
    high = matrix.astype(bf16)
    low = (matrix - high.astype(np.float32)).astype(bf16)
    return pl.pallas_call(
        diffusion_kernel,
        out_shape=jax.ShapeDtypeStruct((3, count, length, NZ), f32),
        compiler_params=pltpu.CompilerParams(vmem_limit_bytes=32 << 20),
        name="diffuse",
    )(jnp.asarray(high), jnp.asarray(low), lines)


def per_device(right_side, class_map, conductivity_table, velocity):
    nx, ny = lax.axis_size("sx"), lax.axis_size("sy")

    def up(peers):
        return [(i, i + 1) for i in range(peers - 1)]

    def down(peers):
        return [(i + 1, i) for i in range(peers - 1)]

    odd = (lax.axis_index("sy") % 2).astype(jnp.int32).reshape(1)
    first, second, low, high = message_of(odd, conductivity_table, right_side, class_map)

    def pairs(start):
        firsts = range(start, ny - 1, 2)
        return [(i, i + 1) for i in firsts] + [(i + 1, i) for i in firsts]

    ya = lax.ppermute(first, "sy", pairs(0))
    yb = lax.ppermute(second, "sy", pairs(1))

    def strip(own, at, next_at, k):
        pieces = [own]
        pieces += [m[at : at + REACH] for m in (ya, yb)]
        pieces += [m[NEAR + next_at : NEAR + next_at + 3] for m in (ya, yb)]
        for m in (ya, yb):
            pieces += [m[NEAR + NEXT + 2 * h + k :][:1] for h in range(2)]
        return jnp.concatenate(pieces, axis=0)

    xl = lax.ppermute(strip(high, CX - REACH, 5, 1), "sx", up(nx))
    xr = lax.ppermute(strip(low, 0, 0, 0), "sx", down(nx))
    d1, e, cond, sums = krylov(ny, odd, right_side, first, ya, yb, xl, xr)
    sums = lax.all_to_all(sums, "sy", split_axis=0, concat_axis=0, tiled=True)
    sums = jnp.broadcast_to(jnp.sum(sums, axis=0, keepdims=True), (nx, 1, NZ))
    sums = lax.all_to_all(sums, "sx", split_axis=0, concat_axis=0, tiled=True)
    potential, moved = velocity_step(sums, d1, e, cond, velocity)
    lines = lax.all_to_all(
        moved.reshape(ny, CX // ny, 3, CY, NZ), "sy", split_axis=0, concat_axis=0, tiled=True
    )
    return potential, diffuse(lines, CY)


def solution(mesh):
    return jax.shard_map(
        per_device,
        mesh=mesh,
        in_specs=(P("sx", "sy", None), P("sx", "sy", None), P(), P(None, "sx", "sy", None)),
        out_specs=(P("sx", "sy", None), P(None, ("sx", "sy"), None, None)),
        check_vma=False,
    )
```

```python
import functools

import jax
import jax.numpy as jnp
import numpy as np
from jax import lax
from jax.experimental import pallas as pl
from jax.experimental.pallas import tpu as pltpu
from jax.sharding import PartitionSpec as P

CX, CY, NZ = 32, 16, 128
CLASSES = 8
PAD = 12
REACH = 10
WX, WY = CX + 2 * PAD, CY + 2 * PAD
EX = 68
EY = 56
AXIAL = 1.0 / 16.0
COUPLING = 0.25
GROUP, GROUP_C, GROUP_I, GROUP_P = 40, 13, 21, 16
f32 = jnp.float32
bf16 = jnp.bfloat16


def lay_out(row):
    return jnp.concatenate([row[0:16], row[8:32], row[24:40]], axis=0)


def gather_middle(row, low):
    return jnp.concatenate(
        [
            jnp.where(low, row[0:8], row[8:16]),
            row[16:24],
            jnp.where(low, row[24:32], row[32:40]),
        ],
        axis=0,
    )


def gather_owned(row, low):
    return jnp.concatenate([row[0:8], gather_middle(row[8:48], low), row[48:56]], axis=0)


def up_y(v):
    return pltpu.roll(v, v.shape[0] - 1, 0)


def down_y(v):
    return pltpu.roll(v, 1, 0)


def up_z(v):
    return pltpu.roll(v, v.shape[1] - 1, 1)


def down_z(v):
    return pltpu.roll(v, 1, 1)


def operator_row(s_ref, v_ref, xw, first, last):
    sl = slice(first, last)
    s, v = s_ref[xw, sl, :], v_ref[xw, sl, :]
    lane = lax.broadcasted_iota(jnp.int32, s.shape, 1)
    not_top, not_bottom = lane < NZ - 1, lane > 0
    total = (s + s_ref[xw + 1, sl, :]) * (v - v_ref[xw + 1, sl, :])
    total = total + (s + s_ref[xw - 1, sl, :]) * (v - v_ref[xw - 1, sl, :])
    total = total + (s + up_y(s)) * (v - up_y(v))
    total = total + (s + down_y(s)) * (v - down_y(v))
    axial = (s + jnp.where(not_top, up_z(s), 0.0)) * (v - jnp.where(not_top, up_z(v), 0.0))
    axial = axial + (s + jnp.where(not_bottom, down_z(s), 0.0)) * (
        v - jnp.where(not_bottom, down_z(v), 0.0)
    )
    return 0.5 * total + (0.5 * AXIAL) * axial


def loop(start, stop, body, group=1):
    whole = (stop - start) // group

    def step(k, carry):
        body(start + k * group, group)
        return carry

    if whole > 1:
        lax.fori_loop(0, whole, step, 0)
    elif whole == 1:
        body(start, group)
    if start + whole * group < stop:
        body(start + whole * group, stop - start - whole * group)


NEAR, NEXT, COND = 32, 8, 4
ALONG_Y = NEAR + NEXT + COND


def message_kernel(
    odd_ref, table_ref, side_ref, class_ref, first_ref, second_ref, low_ref, high_ref
):
    def sides(up_ref, down_ref):
        up_ref[0:CX] = side_ref[:, 8:16, :]
        down_ref[0:CX] = side_ref[:, 0:8, :]
        for x in range(CX):
            at = slice(2 * (x % 4), 2 * (x % 4) + 2)
            up_ref[NEAR + x // 4, at, :] = side_ref[x, 6:8, :]
            down_ref[NEAR + x // 4, at, :] = side_ref[x, 8:10, :]

    @pl.when(odd_ref[0] == 0)
    def _():
        sides(first_ref, second_ref)

    @pl.when(odd_ref[0] == 1)
    def _():
        sides(second_ref, first_ref)

    low_ref[0 : 2 * REACH] = side_ref[0:REACH].reshape(2 * REACH, 8, NZ)
    high_ref[0 : 2 * REACH] = side_ref[CX - REACH : CX].reshape(2 * REACH, 8, NZ)
    for h in range(2):
        classes = jnp.concatenate([class_ref[:, 4 * h + m, :] for m in range(4)], axis=1)
        cond = jnp.zeros(classes.shape, f32)
        for k in range(CLASSES):
            cond = jnp.where(classes == k, table_ref[k], cond)
        for k in range(2):
            tile = cond[8 * k : 8 * k + 8]
            first_ref[NEAR + NEXT + 2 * h + k] = tile
            second_ref[NEAR + NEXT + 2 * h + k] = tile
            (low_ref, high_ref)[k][2 * REACH + h] = tile


def message_of(odd, table, right_side, class_map):
    vmem = pl.BlockSpec(memory_space=pltpu.VMEM)
    smem = pl.BlockSpec(memory_space=pltpu.SMEM)
    along_y = jax.ShapeDtypeStruct((ALONG_Y, 8, NZ), f32)
    along_x = jax.ShapeDtypeStruct((2 * REACH + 2, 8, NZ), f32)
    return pl.pallas_call(
        message_kernel,
        in_specs=[smem, smem, vmem, vmem],
        out_shape=(along_y, along_y, along_x, along_x),
        name="message",
    )(odd, table, right_side, class_map)


def krylov_kernel(
    copies,
    odd_ref,
    own_ref,
    mine_ref,
    ya_ref,
    yb_ref,
    xl_ref,
    xr_ref,
    spread_ref,
    d1_out,
    e_out,
    s_out,
    sums_out,
    sr,
    sa,
    sw,
    rw,
    d1w,
    i1w,
    ew,
    cxp,
    cxm,
    cyp,
    cym,
    czp,
    czm,
    inv,
    t0,
    ta,
    tb,
):
    half = PAD // 2

    def place(at, rows, own, first, near_l, near_r, next_l, next_r):
        rw[at : at + rows, PAD : PAD + CY, :] = own
        rw[at : at + rows, PAD - 8 : PAD, :] = near_l
        rw[at : at + rows, PAD + CY : PAD + CY + 8, :] = near_r
        rw[at : at + rows, 0:2, :] = jnp.zeros((rows, 2, NZ), f32)
        rw[at : at + rows, WY - 2 : WY, :] = jnp.zeros((rows, 2, NZ), f32)
        for i in range(rows):
            x = first + i
            tile, lines = x // 4 - first // 4, slice(2 * (x % 4), 2 * (x % 4) + 2)
            for (ref, start), to in ((next_l, PAD - 10), (next_r, PAD + CY + 8)):
                rw[at + i, to : to + 2, :] = ref[start + tile, lines, :]

    def unpack(yl_ref, yr_ref, l, r):
        for h in range(2):
            for k, ref in enumerate((yl_ref, mine_ref, yr_ref)):
                at = NEAR + NEXT + 2 * h
                sr[k, h, half : half + 8, :] = ref[at]
                sr[k, h, half + 8 : half + 16, :] = ref[at + 1]
            for k, at in enumerate((48 + 2 * l, 20, 48 + 2 * r)):
                sr[k, h, 0:half, :] = xl_ref[at + h, 8 - half : 8, :]
                sr[k, h, half + 16 : 2 * half + 16, :] = xr_ref[at + h, 0:half, :]
        next_y = (yl_ref, NEAR), (yr_ref, NEAR)
        place(PAD, CX, own_ref[...], 0, yl_ref[0:CX], yr_ref[0:CX], *next_y)
        for ref, at, first in ((xl_ref, PAD - REACH, CX - REACH), (xr_ref, PAD + CX, 0)):
            own = ref[0 : 2 * REACH].reshape(REACH, CY, NZ)
            near_l, near_r = (ref[22 + 10 * k : 32 + 10 * k] for k in (l, r))
            place(at, REACH, own, first, near_l, near_r, (ref, 42 + 3 * l), (ref, 42 + 3 * r))

    @pl.when(odd_ref[0] == 0)
    def _():
        unpack(yb_ref, ya_ref, 1, 0)

    @pl.when(odd_ref[0] == 1)
    def _():
        unpack(ya_ref, yb_ref, 0, 1)

    sub = lax.broadcasted_iota(jnp.int32, (8, NZ), 0)
    lane8 = lax.broadcasted_iota(jnp.int32, (8, NZ), 1)
    low8 = sub < 4
    pick = lane8 // 32 == (sub // 2 + 2) % 4

    def spread_row(cx):
        def wide_row(part, h):
            return jnp.broadcast_to(sr[part, h, pl.ds(cx, 1), :], (8, NZ))

        pairs = (
            (wide_row(0, 0), wide_row(0, 1)),
            (wide_row(0, 1), wide_row(1, 0)),
            (wide_row(1, 0), wide_row(1, 1)),
            (wide_row(1, 1), wide_row(2, 0)),
            (wide_row(2, 0), wide_row(2, 1)),
        )
        for t, (a, b) in enumerate(pairs):
            sa[cx, 8 * t : 8 * t + 8, :] = jnp.where(pick, jnp.where(low8, a, b), 0.0)

    def spread_rows(cx, n):
        for i in range(n):
            spread_row(cx + i)

    loop(0, WX // 2, spread_rows, 4)
    spread = spread_ref[...]

    def spread_cells(c, _):
        rest = sa[pl.ds(7 * c, 7), :, :].reshape(7 * WY, NZ)
        out = jnp.zeros((7 * WY, NZ), f32)
        for _ in range(3):
            part = rest.astype(bf16)
            rest = rest - part.astype(f32)
            out = out + jnp.dot(part, spread, preferred_element_type=f32)
        out = out.reshape(7, WY, NZ)
        for k in range(7):
            sw[14 * c + 2 * k, :, :] = out[k]
            sw[14 * c + 2 * k + 1, :, :] = out[k]

    loop(0, 4, spread_cells)

    def coefficient_row(e, xw, cut_up=False, cut_down=False):
        s5 = sw[xw]
        lane = lax.broadcasted_iota(jnp.int32, (WY, NZ), 1)
        place = lax.broadcasted_iota(jnp.int32, (EY, NZ), 0)
        zp = AXIAL * (s5 + jnp.where(lane < NZ - 1, up_z(s5), 0.0))
        zm = AXIAL * (s5 + jnp.where(lane > 0, down_z(s5), 0.0))
        axial = lay_out(zp + zm)
        s = lay_out(s5)
        yp = s + jnp.where((place == 15) | (place == 39), 0.0, lay_out(up_y(s5)))
        ym = s + jnp.where((place == 16) | (place == 40), 0.0, lay_out(down_y(s5)))
        xp = s if cut_up else s + lay_out(sw[xw + 1])
        xm = s if cut_down else s + lay_out(sw[xw - 1])
        inverse = jnp.where(s > 0.0, 1.0 / (xp + xm + yp + ym + axial), 0.0)
        cxp[e] = xp * inverse
        cxm[e] = xm * inverse
        cyp[e] = yp * inverse
        cym[e] = ym * inverse
        czp[e] = lay_out(jnp.where(lane < NZ - 1, zp, 0.0)) * inverse
        czm[e] = lay_out(jnp.where(lane > 0, zm, 0.0)) * inverse
        inverse = inverse + inverse
        inv[e] = inverse
        t0[e] = lay_out(rw[xw]) * inverse

    def coefficient_rows(shift):
        def rows(e, n):
            for i in range(n):
                coefficient_row(e + i, e + i + shift)

        return rows

    loop(0, 13, coefficient_rows(2), GROUP_C)
    coefficient_row(13, 15, cut_up=True)
    coefficient_row(14, 8, cut_down=True)
    loop(15, 53, coefficient_rows(-6), GROUP_C)
    coefficient_row(53, 47, cut_up=True)
    coefficient_row(54, 40, cut_down=True)
    loop(55, EX, coefficient_rows(-14), GROUP_C)

    low = lax.broadcasted_iota(jnp.int32, (8, NZ), 0) < 4

    def swept(src, e, n, narrow):
        lines = slice(8, 48) if narrow else slice(0, EY)
        wider = narrow and src is t0

        def beside(i):
            if not wider:
                return up_y(rows[i]), down_y(rows[i])
            t = src[e - 1 + i]
            return up_y(t)[8:48], down_y(t)[8:48]

        rows = [src[e - 1 + i, lines, :] for i in range(n + 2)]
        out = []
        for i in range(n):
            t = rows[i + 1]
            above, below = beside(i + 1)
            a = t0[e + i, lines, :] + cxp[e + i, lines, :] * rows[i + 2]
            b = cyp[e + i, lines, :] * above + cym[e + i, lines, :] * below
            c = czp[e + i, lines, :] * up_z(t) + czm[e + i, lines, :] * down_z(t)
            out.append((a + cxm[e + i, lines, :] * rows[i]) + (b + c))
        return out

    def sweep(src, dst, ranges, narrow):
        lines = slice(8, 48) if narrow else slice(0, EY)

        def rows(e, n):
            for i, new in enumerate(swept(src, e, n, narrow)):
                dst[e + i, lines, :] = new

        for start, stop, _ in ranges:
            loop(start, stop, rows, GROUP)

    def last_sweep(src, dst, ranges, narrow):
        for start, stop, shift in ranges:

            def rows(e, n, shift=shift):
                for i, new in enumerate(swept(src, e, n, narrow)):
                    if narrow:
                        dst[e + shift + i, 8:32, :] = gather_middle(new, low)
                    else:
                        dst[e + shift + i] = gather_owned(new, low)

            loop(start, stop, rows, GROUP)

    def ranges(k, skip):
        return (
            (skip + k, 14 - k, 2),
            (14 + k, 54 - k, -6),
            (54 + k, EX - skip - k, -14),
        )

    def precondition(dst, skip, narrow):
        sweep(t0, ta, ranges(1, skip), narrow)
        sweep(ta, tb, ranges(2, skip), narrow)
        sweep(tb, ta, ranges(3, skip), narrow)
        last_sweep(ta, dst, ranges(4, skip), narrow)

    precondition(d1w, 0, False)

    def image_rows(xw, n):
        for i, new in enumerate([operator_row(sw, d1w, xw + i, 0, WY) for i in range(n)]):
            i1w[xw + i] = new

    loop(PAD - 5, PAD + CX + 5, image_rows, GROUP_I)

    for start, stop, shift in ranges(0, 5):

        def start_rows(e, n, shift=shift):
            for i in range(n):
                t0[e + i] = lay_out(i1w[e + shift + i]) * inv[e + i]

        loop(start, stop, start_rows, 10)
    precondition(ew, 5, True)

    place = lax.broadcasted_iota(jnp.int32, (24, NZ), 0)
    owned = (place >= 4) & (place < 20)

    def products(xw, sums):
        j = jnp.where(owned, operator_row(sw, ew, xw, 8, 32), 0.0)
        i1 = jnp.where(owned, i1w[xw, 8:32, :], 0.0)
        r = rw[xw, 8:32, :]

        def fold(v):
            return v[0:8] + v[8:16] + v[16:24]

        terms = (r * i1, i1 * i1, i1 * j, r * j, j * j)
        return tuple(acc + fold(t) for acc, t in zip(sums, terms))

    def product_rows(k, sums):
        for i in range(GROUP_P):
            sums = products(PAD + GROUP_P * k + i, sums)
        return sums

    zero = jnp.zeros((8, NZ), f32)
    sums = lax.fori_loop(0, CX // GROUP_P, product_rows, (zero,) * 5)
    block = jnp.zeros((1, NZ), f32)
    for k, acc in enumerate(sums):
        total = jnp.sum(jnp.sum(acc, axis=0, keepdims=True), axis=1, keepdims=True)
        block = jnp.where(lane8[0:1] == k, total, block)
    for k in range(copies):
        sums_out[k] = block
    d1_out[...] = d1w[PAD - 1 : PAD + CX + 1, 8:32, :]
    e_out[...] = ew[PAD - 1 : PAD + CX + 1, 8:32, :]
    s_out[...] = sw[PAD : PAD + CX, 8:32, :]


def krylov(copies, odd, own, mine, ya, yb, xl, xr):
    smem, vmem = (pl.BlockSpec(memory_space=m) for m in (pltpu.SMEM, pltpu.VMEM))
    lane = np.arange(NZ)
    spread = jnp.asarray((lane[:, None] % 32 == lane[None, :] // 4).astype(np.float32), bf16)
    wide = pltpu.VMEM((WX, WY, NZ), f32)
    laid = pltpu.VMEM((EX, EY, NZ), f32)
    return pl.pallas_call(
        functools.partial(krylov_kernel, copies),
        in_specs=[smem] + [vmem] * 7,
        out_shape=(
            jax.ShapeDtypeStruct((CX + 2, 24, NZ), f32),
            jax.ShapeDtypeStruct((CX + 2, 24, NZ), f32),
            jax.ShapeDtypeStruct((CX, 24, NZ), f32),
            jax.ShapeDtypeStruct((copies, 1, NZ), f32),
        ),
        scratch_shapes=[
            pltpu.VMEM((3, 2, WX // 2, NZ), f32),
            pltpu.VMEM((WX // 2, WY, NZ), f32),
            wide,
            wide,
            wide,
            wide,
            wide,
        ]
        + [laid] * 10,
        compiler_params=pltpu.CompilerParams(vmem_limit_bytes=48 << 20),
        name="krylov",
    )(odd, own, mine, ya, yb, xl, xr, spread)


def velocity_kernel(parts_ref, d1_ref, e_ref, s_ref, v_ref, pot_ref, moved_ref):
    totals = jnp.sum(parts_ref[...], axis=0)
    lane = lax.broadcasted_iota(jnp.int32, (1, NZ), 1)
    a, b, c, d, g = (
        jnp.sum(jnp.where(lane == k, totals, 0.0), axis=1, keepdims=True) for k in range(5)
    )
    ratio = c / b
    second = (d - ratio * a) / (g - ratio * c)
    first = a / b - ratio * second
    p1 = jnp.broadcast_to(first, (24, NZ))
    p2 = jnp.broadcast_to(second, (24, NZ))

    def row(i, before_here):
        before, here = before_here
        after = p1 * d1_ref[i + 2] + p2 * e_ref[i + 2]
        factor = COUPLING * s_ref[i]
        grad_x = 0.5 * (after - before)
        grad_y = 0.5 * (up_y(here) - down_y(here))
        pot_ref[i] = here[4:20]
        vx, vy = v_ref[0, i], v_ref[1, i]
        force_y = (factor * grad_x)[4:20]
        force_x = (factor * grad_y)[4:20]
        factor = factor[4:20]
        moved_ref[i, 0] = vx - force_x - factor * vx
        moved_ref[i, 1] = vy + force_y - factor * vy
        moved_ref[i, 2] = v_ref[2, i]
        return here, after

    lax.fori_loop(
        0, CX, row, (p1 * d1_ref[0] + p2 * e_ref[0], p1 * d1_ref[1] + p2 * e_ref[1])
    )


def velocity_step(parts, d1, e, cond, velocity):
    return pl.pallas_call(
        velocity_kernel,
        out_shape=(
            jax.ShapeDtypeStruct((CX, CY, NZ), f32),
            jax.ShapeDtypeStruct((CX, 3, CY, NZ), f32),
        ),
        compiler_params=pltpu.CompilerParams(vmem_limit_bytes=32 << 20),
        name="velocity_step",
    )(parts, d1, e, cond, velocity)


def diffusion_matrix(lines_count, cells_side):
    k = np.arange(lines_count) + 1
    phase = (k[:, None] * k[None, :]) % (2 * (lines_count + 1))
    sine = np.sqrt(2.0 / (lines_count + 1)) * np.sin(np.pi * phase / (lines_count + 1))
    half = np.sin(0.5 * np.pi * k / (lines_count + 1))
    gain = 2.0 / (1.0 + 8.0 * cells_side * cells_side * half * half)
    return (sine * gain) @ sine


def diffusion_kernel(high_ref, low_ref, x_ref, out_ref):
    high, low = high_ref[...], low_ref[...]
    for i in range(x_ref.shape[1]):
        parts = [x_ref[:, i, c, :, :].reshape(high.shape[0], NZ) for c in range(3)]
        x = jnp.concatenate(parts, axis=1)
        big = x.astype(bf16)
        small = (x - big.astype(f32)).astype(bf16)
        total = jnp.dot(high, small, preferred_element_type=f32)
        total = total + jnp.dot(low, big, preferred_element_type=f32)
        total = total + jnp.dot(high, big, preferred_element_type=f32)
        for c in range(3):
            out_ref[c, i] = total[:, NZ * c : NZ * (c + 1)] - parts[c]


def diffuse(lines, cells_side):
    sources, count = lines.shape[0], lines.shape[1]
    length = sources * cells_side
    matrix = diffusion_matrix(length, cells_side).astype(np.float32)
    high = matrix.astype(bf16)
    low = (matrix - high.astype(np.float32)).astype(bf16)
    return pl.pallas_call(
        diffusion_kernel,
        out_shape=jax.ShapeDtypeStruct((3, count, length, NZ), f32),
        compiler_params=pltpu.CompilerParams(vmem_limit_bytes=32 << 20),
        name="diffuse",
    )(jnp.asarray(high), jnp.asarray(low), lines)


def per_device(right_side, class_map, conductivity_table, velocity):
    nx, ny = lax.axis_size("sx"), lax.axis_size("sy")

    def up(peers):
        return [(i, i + 1) for i in range(peers - 1)]

    def down(peers):
        return [(i + 1, i) for i in range(peers - 1)]

    odd = (lax.axis_index("sy") % 2).astype(jnp.int32).reshape(1)
    first, second, low, high = message_of(odd, conductivity_table, right_side, class_map)

    def pairs(start):
        firsts = range(start, ny - 1, 2)
        return [(i, i + 1) for i in firsts] + [(i + 1, i) for i in firsts]

    ya = lax.ppermute(first, "sy", pairs(0))
    yb = lax.ppermute(second, "sy", pairs(1))

    def strip(own, at, next_at, k):
        pieces = [own]
        pieces += [m[at : at + REACH] for m in (ya, yb)]
        pieces += [m[NEAR + next_at : NEAR + next_at + 3] for m in (ya, yb)]
        for m in (ya, yb):
            pieces += [m[NEAR + NEXT + 2 * h + k :][:1] for h in range(2)]
        return jnp.concatenate(pieces, axis=0)

    xl = lax.ppermute(strip(high, CX - REACH, 5, 1), "sx", up(nx))
    xr = lax.ppermute(strip(low, 0, 0, 0), "sx", down(nx))
    d1, e, cond, sums = krylov(ny, odd, right_side, first, ya, yb, xl, xr)
    sums = lax.all_to_all(sums, "sy", split_axis=0, concat_axis=0, tiled=True)
    sums = jnp.broadcast_to(jnp.sum(sums, axis=0, keepdims=True), (nx, 1, NZ))
    sums = lax.all_to_all(sums, "sx", split_axis=0, concat_axis=0, tiled=True)
    potential, moved = velocity_step(sums, d1, e, cond, velocity)
    lines = lax.all_to_all(
        moved.reshape(ny, CX // ny, 3, CY, NZ), "sy", split_axis=0, concat_axis=0, tiled=True
    )
    return potential, diffuse(lines, CY)


def solution(mesh):
    return jax.shard_map(
        per_device,
        mesh=mesh,
        in_specs=(P("sx", "sy", None), P("sx", "sy", None), P(), P(None, "sx", "sy", None)),
        out_specs=(P("sx", "sy", None), P(None, ("sx", "sy"), None, None)),
        check_vma=False,
    )
```

```python
import functools

import jax
import jax.numpy as jnp
import numpy as np
from jax import lax
from jax.experimental import pallas as pl
from jax.experimental.pallas import tpu as pltpu
from jax.sharding import PartitionSpec as P

CX, CY, NZ = 32, 16, 128
CLASSES = 8
PAD = 12
REACH = 10
WX, WY = CX + 2 * PAD, CY + 2 * PAD
EX = 68
EY = 56
AXIAL = 1.0 / 16.0
COUPLING = 0.25
GROUP, GROUP_C, GROUP_I, GROUP_P = 40, 13, 21, 16
f32 = jnp.float32
bf16 = jnp.bfloat16


def lay_out(row):
    return jnp.concatenate([row[0:16], row[8:32], row[24:40]], axis=0)


def gather_middle(row, low):
    return jnp.concatenate(
        [
            jnp.where(low, row[0:8], row[8:16]),
            row[16:24],
            jnp.where(low, row[24:32], row[32:40]),
        ],
        axis=0,
    )


def gather_owned(row, low):
    return jnp.concatenate([row[0:8], gather_middle(row[8:48], low), row[48:56]], axis=0)


def up_y(v):
    return pltpu.roll(v, v.shape[0] - 1, 0)


def down_y(v):
    return pltpu.roll(v, 1, 0)


def up_z(v):
    return pltpu.roll(v, v.shape[1] - 1, 1)


def down_z(v):
    return pltpu.roll(v, 1, 1)


def operator_row(s_ref, v_ref, xw, first, last):
    sl = slice(first, last)
    s, v = s_ref[xw, sl, :], v_ref[xw, sl, :]
    lane = lax.broadcasted_iota(jnp.int32, s.shape, 1)
    not_top, not_bottom = lane < NZ - 1, lane > 0
    total = (s + s_ref[xw + 1, sl, :]) * (v - v_ref[xw + 1, sl, :])
    total = total + (s + s_ref[xw - 1, sl, :]) * (v - v_ref[xw - 1, sl, :])
    total = total + (s + up_y(s)) * (v - up_y(v))
    total = total + (s + down_y(s)) * (v - down_y(v))
    axial = (s + jnp.where(not_top, up_z(s), 0.0)) * (v - jnp.where(not_top, up_z(v), 0.0))
    axial = axial + (s + jnp.where(not_bottom, down_z(s), 0.0)) * (
        v - jnp.where(not_bottom, down_z(v), 0.0)
    )
    return 0.5 * total + (0.5 * AXIAL) * axial


def loop(start, stop, body, group=1):
    whole = (stop - start) // group

    def step(k, carry):
        body(start + k * group, group)
        return carry

    if whole > 1:
        lax.fori_loop(0, whole, step, 0)
    elif whole == 1:
        body(start, group)
    if start + whole * group < stop:
        body(start + whole * group, stop - start - whole * group)


NEAR, NEXT, COND = 32, 8, 4
ALONG_Y = NEAR + NEXT + COND


def message_kernel(
    odd_ref, table_ref, side_ref, class_ref, first_ref, second_ref, low_ref, high_ref
):
    def sides(up_ref, down_ref):
        up_ref[0:CX] = side_ref[:, 8:16, :]
        down_ref[0:CX] = side_ref[:, 0:8, :]
        for x in range(CX):
            at = slice(2 * (x % 4), 2 * (x % 4) + 2)
            up_ref[NEAR + x // 4, at, :] = side_ref[x, 6:8, :]
            down_ref[NEAR + x // 4, at, :] = side_ref[x, 8:10, :]

    @pl.when(odd_ref[0] == 0)
    def _():
        sides(first_ref, second_ref)

    @pl.when(odd_ref[0] == 1)
    def _():
        sides(second_ref, first_ref)

    low_ref[0 : 2 * REACH] = side_ref[0:REACH].reshape(2 * REACH, 8, NZ)
    high_ref[0 : 2 * REACH] = side_ref[CX - REACH : CX].reshape(2 * REACH, 8, NZ)
    for h in range(2):
        classes = jnp.concatenate([class_ref[:, 4 * h + m, :] for m in range(4)], axis=1)
        cond = jnp.zeros(classes.shape, f32)
        for k in range(CLASSES):
            cond = jnp.where(classes == k, table_ref[k], cond)
        for k in range(2):
            tile = cond[8 * k : 8 * k + 8]
            first_ref[NEAR + NEXT + 2 * h + k] = tile
            second_ref[NEAR + NEXT + 2 * h + k] = tile
            (low_ref, high_ref)[k][2 * REACH + h] = tile


def message_of(odd, table, right_side, class_map):
    vmem = pl.BlockSpec(memory_space=pltpu.VMEM)
    smem = pl.BlockSpec(memory_space=pltpu.SMEM)
    along_y = jax.ShapeDtypeStruct((ALONG_Y, 8, NZ), f32)
    along_x = jax.ShapeDtypeStruct((2 * REACH + 2, 8, NZ), f32)
    return pl.pallas_call(
        message_kernel,
        in_specs=[smem, smem, vmem, vmem],
        out_shape=(along_y, along_y, along_x, along_x),
        name="message",
    )(odd, table, right_side, class_map)


def krylov_kernel(
    copies,
    odd_ref,
    own_ref,
    mine_ref,
    ya_ref,
    yb_ref,
    xl_ref,
    xr_ref,
    spread_ref,
    d1_out,
    e_out,
    s_out,
    sums_out,
    sr,
    sa,
    sw,
    rw,
    d1w,
    i1w,
    ew,
    cxp,
    cxm,
    cyp,
    cym,
    czp,
    czm,
    inv,
    t0,
    ta,
    tb,
):
    half = PAD // 2

    def place(at, rows, own, first, near_l, near_r, next_l, next_r):
        rw[at : at + rows, PAD : PAD + CY, :] = own
        rw[at : at + rows, PAD - 8 : PAD, :] = near_l
        rw[at : at + rows, PAD + CY : PAD + CY + 8, :] = near_r
        rw[at : at + rows, 0:2, :] = jnp.zeros((rows, 2, NZ), f32)
        rw[at : at + rows, WY - 2 : WY, :] = jnp.zeros((rows, 2, NZ), f32)
        for i in range(rows):
            x = first + i
            tile, lines = x // 4 - first // 4, slice(2 * (x % 4), 2 * (x % 4) + 2)
            for (ref, start), to in ((next_l, PAD - 10), (next_r, PAD + CY + 8)):
                rw[at + i, to : to + 2, :] = ref[start + tile, lines, :]

    def unpack(yl_ref, yr_ref, l, r):
        for h in range(2):
            for k, ref in enumerate((yl_ref, mine_ref, yr_ref)):
                at = NEAR + NEXT + 2 * h
                sr[k, h, half : half + 8, :] = ref[at]
                sr[k, h, half + 8 : half + 16, :] = ref[at + 1]
            for k, at in enumerate((48 + 2 * l, 20, 48 + 2 * r)):
                sr[k, h, 0:half, :] = xl_ref[at + h, 8 - half : 8, :]
                sr[k, h, half + 16 : 2 * half + 16, :] = xr_ref[at + h, 0:half, :]
        next_y = (yl_ref, NEAR), (yr_ref, NEAR)
        place(PAD, CX, own_ref[...], 0, yl_ref[0:CX], yr_ref[0:CX], *next_y)
        for ref, at, first in ((xl_ref, PAD - REACH, CX - REACH), (xr_ref, PAD + CX, 0)):
            own = ref[0 : 2 * REACH].reshape(REACH, CY, NZ)
            near_l, near_r = (ref[22 + 10 * k : 32 + 10 * k] for k in (l, r))
            place(at, REACH, own, first, near_l, near_r, (ref, 42 + 3 * l), (ref, 42 + 3 * r))

    @pl.when(odd_ref[0] == 0)
    def _():
        unpack(yb_ref, ya_ref, 1, 0)

    @pl.when(odd_ref[0] == 1)
    def _():
        unpack(ya_ref, yb_ref, 0, 1)

    sub = lax.broadcasted_iota(jnp.int32, (8, NZ), 0)
    lane8 = lax.broadcasted_iota(jnp.int32, (8, NZ), 1)
    low8 = sub < 4
    pick = lane8 // 32 == (sub // 2 + 2) % 4

    def spread_row(cx):
        def wide_row(part, h):
            return jnp.broadcast_to(sr[part, h, pl.ds(cx, 1), :], (8, NZ))

        pairs = (
            (wide_row(0, 0), wide_row(0, 1)),
            (wide_row(0, 1), wide_row(1, 0)),
            (wide_row(1, 0), wide_row(1, 1)),
            (wide_row(1, 1), wide_row(2, 0)),
            (wide_row(2, 0), wide_row(2, 1)),
        )
        for t, (a, b) in enumerate(pairs):
            sa[cx, 8 * t : 8 * t + 8, :] = jnp.where(pick, jnp.where(low8, a, b), 0.0)

    def spread_rows(cx, n):
        for i in range(n):
            spread_row(cx + i)

    loop(0, WX // 2, spread_rows, 4)
    spread = spread_ref[...]

    def spread_cells(c, _):
        rest = sa[pl.ds(7 * c, 7), :, :].reshape(7 * WY, NZ)
        out = jnp.zeros((7 * WY, NZ), f32)
        for _ in range(3):
            part = rest.astype(bf16)
            rest = rest - part.astype(f32)
            out = out + jnp.dot(part, spread, preferred_element_type=f32)
        out = out.reshape(7, WY, NZ)
        for k in range(7):
            sw[14 * c + 2 * k, :, :] = out[k]
            sw[14 * c + 2 * k + 1, :, :] = out[k]

    loop(0, 4, spread_cells)

    def coefficient_row(e, xw, cut_up=False, cut_down=False):
        s5 = sw[xw]
        lane = lax.broadcasted_iota(jnp.int32, (WY, NZ), 1)
        place = lax.broadcasted_iota(jnp.int32, (EY, NZ), 0)
        zp = AXIAL * (s5 + jnp.where(lane < NZ - 1, up_z(s5), 0.0))
        zm = AXIAL * (s5 + jnp.where(lane > 0, down_z(s5), 0.0))
        axial = lay_out(zp + zm)
        s = lay_out(s5)
        yp = s + jnp.where((place == 15) | (place == 39), 0.0, lay_out(up_y(s5)))
        ym = s + jnp.where((place == 16) | (place == 40), 0.0, lay_out(down_y(s5)))
        xp = s if cut_up else s + lay_out(sw[xw + 1])
        xm = s if cut_down else s + lay_out(sw[xw - 1])
        inverse = jnp.where(s > 0.0, 1.0 / (xp + xm + yp + ym + axial), 0.0)
        cxp[e] = xp * inverse
        cxm[e] = xm * inverse
        cyp[e] = yp * inverse
        cym[e] = ym * inverse
        czp[e] = lay_out(jnp.where(lane < NZ - 1, zp, 0.0)) * inverse
        czm[e] = lay_out(jnp.where(lane > 0, zm, 0.0)) * inverse
        inverse = inverse + inverse
        inv[e] = inverse
        t0[e] = lay_out(rw[xw]) * inverse

    def coefficient_rows(shift):
        def rows(e, n):
            for i in range(n):
                coefficient_row(e + i, e + i + shift)

        return rows

    loop(0, 13, coefficient_rows(2), GROUP_C)
    coefficient_row(13, 15, cut_up=True)
    coefficient_row(14, 8, cut_down=True)
    loop(15, 53, coefficient_rows(-6), GROUP_C)
    coefficient_row(53, 47, cut_up=True)
    coefficient_row(54, 40, cut_down=True)
    loop(55, EX, coefficient_rows(-14), GROUP_C)

    low = lax.broadcasted_iota(jnp.int32, (8, NZ), 0) < 4

    def swept(src, e, n, narrow):
        lines = slice(8, 48) if narrow else slice(0, EY)
        wider = narrow and src is t0

        def beside(i):
            if not wider:
                return up_y(rows[i]), down_y(rows[i])
            t = src[e - 1 + i]
            return up_y(t)[8:48], down_y(t)[8:48]

        rows = [src[e - 1 + i, lines, :] for i in range(n + 2)]
        out = []
        for i in range(n):
            t = rows[i + 1]
            above, below = beside(i + 1)
            a = t0[e + i, lines, :] + cxp[e + i, lines, :] * rows[i + 2]
            b = cyp[e + i, lines, :] * above + cym[e + i, lines, :] * below
            c = czp[e + i, lines, :] * up_z(t) + czm[e + i, lines, :] * down_z(t)
            out.append((a + cxm[e + i, lines, :] * rows[i]) + (b + c))
        return out

    def sweep(src, dst, ranges, narrow):
        lines = slice(8, 48) if narrow else slice(0, EY)

        def rows(e, n):
            for i, new in enumerate(swept(src, e, n, narrow)):
                dst[e + i, lines, :] = new

        for start, stop, _ in ranges:
            loop(start, stop, rows, GROUP)

    def last_sweep(src, dst, ranges, narrow):
        for start, stop, shift in ranges:

            def rows(e, n, shift=shift):
                for i, new in enumerate(swept(src, e, n, narrow)):
                    if narrow:
                        dst[e + shift + i, 8:32, :] = gather_middle(new, low)
                    else:
                        dst[e + shift + i] = gather_owned(new, low)

            loop(start, stop, rows, GROUP)

    def ranges(k, skip):
        return (
            (skip + k, 14 - k, 2),
            (14 + k, 54 - k, -6),
            (54 + k, EX - skip - k, -14),
        )

    def precondition(dst, skip, narrow):
        sweep(t0, ta, ranges(1, skip), narrow)
        sweep(ta, tb, ranges(2, skip), narrow)
        sweep(tb, ta, ranges(3, skip), narrow)
        last_sweep(ta, dst, ranges(4, skip), narrow)

    precondition(d1w, 0, False)

    def image_rows(xw, n):
        for i, new in enumerate([operator_row(sw, d1w, xw + i, 0, WY) for i in range(n)]):
            i1w[xw + i] = new

    loop(PAD - 5, PAD + CX + 5, image_rows, GROUP_I)

    for start, stop, shift in ranges(0, 5):

        def start_rows(e, n, shift=shift):
            for i in range(n):
                t0[e + i] = lay_out(i1w[e + shift + i]) * inv[e + i]

        loop(start, stop, start_rows, 10)
    precondition(ew, 5, True)

    place = lax.broadcasted_iota(jnp.int32, (24, NZ), 0)
    owned = (place >= 4) & (place < 20)

    def products(xw, sums):
        j = jnp.where(owned, operator_row(sw, ew, xw, 8, 32), 0.0)
        i1 = jnp.where(owned, i1w[xw, 8:32, :], 0.0)
        r = rw[xw, 8:32, :]

        def fold(v):
            return v[0:8] + v[8:16] + v[16:24]

        terms = (r * i1, i1 * i1, i1 * j, r * j, j * j)
        return tuple(acc + fold(t) for acc, t in zip(sums, terms))

    def product_rows(k, sums):
        for i in range(GROUP_P):
            sums = products(PAD + GROUP_P * k + i, sums)
        return sums

    zero = jnp.zeros((8, NZ), f32)
    sums = lax.fori_loop(0, CX // GROUP_P, product_rows, (zero,) * 5)
    block = jnp.zeros((1, NZ), f32)
    for k, acc in enumerate(sums):
        total = jnp.sum(jnp.sum(acc, axis=0, keepdims=True), axis=1, keepdims=True)
        block = jnp.where(lane8[0:1] == k, total, block)
    for k in range(copies):
        sums_out[k] = block
    d1_out[...] = d1w[PAD - 1 : PAD + CX + 1, 8:32, :]
    e_out[...] = ew[PAD - 1 : PAD + CX + 1, 8:32, :]
    s_out[...] = sw[PAD : PAD + CX, 8:32, :]


def krylov(copies, odd, own, mine, ya, yb, xl, xr):
    smem, vmem = (pl.BlockSpec(memory_space=m) for m in (pltpu.SMEM, pltpu.VMEM))
    lane = np.arange(NZ)
    spread = jnp.asarray((lane[:, None] % 32 == lane[None, :] // 4).astype(np.float32), bf16)
    wide = pltpu.VMEM((WX, WY, NZ), f32)
    laid = pltpu.VMEM((EX, EY, NZ), f32)
    return pl.pallas_call(
        functools.partial(krylov_kernel, copies),
        in_specs=[smem] + [vmem] * 7,
        out_shape=(
            jax.ShapeDtypeStruct((CX + 2, 24, NZ), f32),
            jax.ShapeDtypeStruct((CX + 2, 24, NZ), f32),
            jax.ShapeDtypeStruct((CX, 24, NZ), f32),
            jax.ShapeDtypeStruct((copies, 1, NZ), f32),
        ),
        scratch_shapes=[
            pltpu.VMEM((3, 2, WX // 2, NZ), f32),
            pltpu.VMEM((WX // 2, WY, NZ), f32),
            wide,
            wide,
            wide,
            wide,
            wide,
        ]
        + [laid] * 10,
        compiler_params=pltpu.CompilerParams(vmem_limit_bytes=48 << 20),
        name="krylov",
    )(odd, own, mine, ya, yb, xl, xr, spread)


def velocity_kernel(parts_ref, d1_ref, e_ref, s_ref, v_ref, pot_ref, moved_ref):
    totals = jnp.sum(parts_ref[...], axis=0)
    lane = lax.broadcasted_iota(jnp.int32, (1, NZ), 1)
    a, b, c, d, g = (
        jnp.sum(jnp.where(lane == k, totals, 0.0), axis=1, keepdims=True) for k in range(5)
    )
    ratio = c / b
    second = (d - ratio * a) / (g - ratio * c)
    first = a / b - ratio * second
    p1 = jnp.broadcast_to(first, (24, NZ))
    p2 = jnp.broadcast_to(second, (24, NZ))

    def row(i, before_here):
        before, here = before_here
        after = p1 * d1_ref[i + 2] + p2 * e_ref[i + 2]
        factor = COUPLING * s_ref[i]
        grad_x = 0.5 * (after - before)
        grad_y = 0.5 * (up_y(here) - down_y(here))
        pot_ref[i] = here[4:20]
        vx, vy = v_ref[0, i], v_ref[1, i]
        force_y = (factor * grad_x)[4:20]
        force_x = (factor * grad_y)[4:20]
        factor = factor[4:20]
        moved_ref[i, 0] = vx - force_x - factor * vx
        moved_ref[i, 1] = vy + force_y - factor * vy
        moved_ref[i, 2] = v_ref[2, i]
        return here, after

    def rows(k, before_here):
        for i in range(8):
            before_here = row(8 * k + i, before_here)
        return before_here

    lax.fori_loop(
        0, CX // 8, rows, (p1 * d1_ref[0] + p2 * e_ref[0], p1 * d1_ref[1] + p2 * e_ref[1])
    )


def velocity_step(parts, d1, e, cond, velocity):
    return pl.pallas_call(
        velocity_kernel,
        out_shape=(
            jax.ShapeDtypeStruct((CX, CY, NZ), f32),
            jax.ShapeDtypeStruct((CX, 3, CY, NZ), f32),
        ),
        compiler_params=pltpu.CompilerParams(vmem_limit_bytes=32 << 20),
        name="velocity_step",
    )(parts, d1, e, cond, velocity)


def diffusion_matrix(lines_count, cells_side):
    k = np.arange(lines_count) + 1
    phase = (k[:, None] * k[None, :]) % (2 * (lines_count + 1))
    sine = np.sqrt(2.0 / (lines_count + 1)) * np.sin(np.pi * phase / (lines_count + 1))
    half = np.sin(0.5 * np.pi * k / (lines_count + 1))
    gain = 2.0 / (1.0 + 8.0 * cells_side * cells_side * half * half)
    return (sine * gain) @ sine


def diffusion_kernel(high_ref, low_ref, x_ref, out_ref):
    high, low = high_ref[...], low_ref[...]
    for i in range(x_ref.shape[1]):
        parts = [x_ref[:, i, c, :, :].reshape(high.shape[0], NZ) for c in range(3)]
        x = jnp.concatenate(parts, axis=1)
        big = x.astype(bf16)
        small = (x - big.astype(f32)).astype(bf16)
        total = jnp.dot(high, small, preferred_element_type=f32)
        total = total + jnp.dot(low, big, preferred_element_type=f32)
        total = total + jnp.dot(high, big, preferred_element_type=f32)
        for c in range(3):
            out_ref[c, i] = total[:, NZ * c : NZ * (c + 1)] - parts[c]


def diffuse(lines, cells_side):
    sources, count = lines.shape[0], lines.shape[1]
    length = sources * cells_side
    matrix = diffusion_matrix(length, cells_side).astype(np.float32)
    high = matrix.astype(bf16)
    low = (matrix - high.astype(np.float32)).astype(bf16)
    return pl.pallas_call(
        diffusion_kernel,
        out_shape=jax.ShapeDtypeStruct((3, count, length, NZ), f32),
        compiler_params=pltpu.CompilerParams(vmem_limit_bytes=32 << 20),
        name="diffuse",
    )(jnp.asarray(high), jnp.asarray(low), lines)


def per_device(right_side, class_map, conductivity_table, velocity):
    nx, ny = lax.axis_size("sx"), lax.axis_size("sy")

    def up(peers):
        return [(i, i + 1) for i in range(peers - 1)]

    def down(peers):
        return [(i + 1, i) for i in range(peers - 1)]

    odd = (lax.axis_index("sy") % 2).astype(jnp.int32).reshape(1)
    first, second, low, high = message_of(odd, conductivity_table, right_side, class_map)

    def pairs(start):
        firsts = range(start, ny - 1, 2)
        return [(i, i + 1) for i in firsts] + [(i + 1, i) for i in firsts]

    ya = lax.ppermute(first, "sy", pairs(0))
    yb = lax.ppermute(second, "sy", pairs(1))

    def strip(own, at, next_at, k):
        pieces = [own]
        pieces += [m[at : at + REACH] for m in (ya, yb)]
        pieces += [m[NEAR + next_at : NEAR + next_at + 3] for m in (ya, yb)]
        for m in (ya, yb):
            pieces += [m[NEAR + NEXT + 2 * h + k :][:1] for h in range(2)]
        return jnp.concatenate(pieces, axis=0)

    xl = lax.ppermute(strip(high, CX - REACH, 5, 1), "sx", up(nx))
    xr = lax.ppermute(strip(low, 0, 0, 0), "sx", down(nx))
    d1, e, cond, sums = krylov(ny, odd, right_side, first, ya, yb, xl, xr)
    sums = lax.all_to_all(sums, "sy", split_axis=0, concat_axis=0, tiled=True)
    sums = jnp.broadcast_to(jnp.sum(sums, axis=0, keepdims=True), (nx, 1, NZ))
    sums = lax.all_to_all(sums, "sx", split_axis=0, concat_axis=0, tiled=True)
    potential, moved = velocity_step(sums, d1, e, cond, velocity)
    lines = lax.all_to_all(
        moved.reshape(ny, CX // ny, 3, CY, NZ), "sy", split_axis=0, concat_axis=0, tiled=True
    )
    return potential, diffuse(lines, CY)


def solution(mesh):
    return jax.shard_map(
        per_device,
        mesh=mesh,
        in_specs=(P("sx", "sy", None), P("sx", "sy", None), P(), P(None, "sx", "sy", None)),
        out_specs=(P("sx", "sy", None), P(None, ("sx", "sy"), None, None)),
        check_vma=False,
    )
```
